32 devices in a mesh: pairs: 2 (over x), blk: 16 (over z, y, core).
Axes of the slice: x: 2, y: 2, z: 4, core: 2. Of those that a mesh axis runs over, the one named last changes fastest.
Arguments:
- src_emb: bfloat16 [32768, 1024], P(('pairs', 'blk')), parts along dimension 0, may hold values from -4 to 4
- src_scale: float32 [32768], P(('pairs', 'blk')), parts along dimension 0, may hold values from 0.3 to 3
- src_count: int32 [32], P(('pairs', 'blk')), parts along dimension 0, may hold values from 512 to 1024, as said below
- tgt_emb: bfloat16 [512, 1024], P(('pairs', 'blk')), parts along dimension 0, may hold values from -4 to 4
- tgt_scale: float32 [512], P(('pairs', 'blk')), parts along dimension 0, may hold values from 0.3 to 3
- tgt_count: int32 [32], P(('pairs', 'blk')), parts along dimension 0, may hold values from 8 to 16, as said below
Outputs:
- best_source: float32 [32768], P(('pairs', 'blk')), parts along dimension 0
- best_target: float32 [512], P(('pairs', 'blk')), parts along dimension 0
The draws below stay inside these ranges and needn't reach their ends.
There are 2 independent parts, one for each index of `pairs`. The reference program is written for one: setup_inputs(seed, part) draws one part's arguments, and reference() takes and returns one part's arrays. A program takes and returns all parts, laid end to end along the dimension named above; each array names one. Nothing has to cross between parts.
Inputs may be any that keep to these rules, and one draw needn't show every extreme that they name: `src_count`: counts the live rows of each block of 1024 source rows, which are its first rows; at least one block is full. `tgt_count`: counts the live rows of each block of 16 target rows, which are its first rows; at least one block is full.
All inputs are finite; a program needn't handle non-finite values.
Results may differ from the reference program's by a relative error of at most 0.0003.
Values may be sent and summed in bfloat16 or wider, within the bound.
No kernel may reach another device: no remote copies, remote signals or barrier semaphores. Data moves between devices by JAX's collectives and lax.ppermute only.
A program may use at most 64 MiB of HBM per device.

```python
import math
import jax
import jax.numpy as jnp
from jax import lax

D = 1024
S_DEV = 1024
T_DEV = 16
S_ROWS = 16384
T_ROWS = 256


pair_count = 6


extra_count = 12


def drawn(key):
    picks = jax.random.fold_in(key, 11)
    source_block = jax.random.permutation(jax.random.fold_in(picks, 1), S_ROWS // S_DEV)[:pair_count]
    source_offset = jax.random.randint(jax.random.fold_in(picks, 3), (pair_count,), 0, S_DEV // 2)
    target_block = jax.random.permutation(jax.random.fold_in(picks, 2), T_ROWS // T_DEV)[:2 * pair_count]
    target_offset = jax.random.randint(jax.random.fold_in(picks, 4), (2 * pair_count,), 0, T_DEV // 2)
    source_pick = (source_block * S_DEV + source_offset).astype(jnp.int32)
    target_pick = (target_block * T_DEV + target_offset).astype(jnp.int32)
    return (source_pick, target_pick)


def drawn_scales(key):
    picks = jax.random.fold_in(key, 12)
    source_level = jax.random.uniform(jax.random.fold_in(picks, 41), (pair_count,), jnp.float32, 2.5, 3.0)
    target_level = jax.random.uniform(jax.random.fold_in(picks, 42), (2 * pair_count,), jnp.float32, 2.5, 2.95)
    extra_rows = jax.random.randint(jax.random.fold_in(picks, 43), (extra_count,), 0, T_ROWS).astype(jnp.int32)
    return (source_level, target_level, extra_rows)


def source_rows(key):
    base = jax.random.truncated_normal(jax.random.fold_in(key, 21), -3.0, 3.0, (S_ROWS, D), jnp.float32)
    col_factor = jax.random.uniform(jax.random.fold_in(key, 25), (D,), jnp.float32, 0.6, 1.1)
    values = base * col_factor[None, :]
    return values


def draw_src_emb(key, part):
    return source_rows(key).astype(jnp.bfloat16)


def draw_tgt_emb(key, part):
    values = jax.random.truncated_normal(jax.random.fold_in(key, 22), -4.0, 4.0, (T_ROWS, D), jnp.float32) / 32.0
    source_pick, target_pick = drawn(key)
    source_level, target_level, extra_rows = drawn_scales(key)
    rounded = source_rows(key)[source_pick].astype(jnp.bfloat16).astype(jnp.float32)
    norms = jnp.sum(rounded * rounded, axis=1)
    base_level = 120.0
    strength = base_level + 60.0 * jnp.arange(pair_count, dtype=jnp.float32)
    first_factor = jnp.minimum(strength / (source_level * target_level[0::2] * norms), 1.0)
    second_factor = jnp.minimum((strength + 2.0) / (source_level * target_level[1::2] * norms), 1.0)
    values = values.at[target_pick[0::2]].set(rounded * first_factor[:, None])
    values = values.at[target_pick[1::2]].set(rounded * second_factor[:, None])
    return values.astype(jnp.bfloat16)


def row_scales(key, length):
    spread = jax.random.uniform(key, (length,), jnp.float32, jnp.log(0.3), jnp.log(3.0))
    return jnp.exp(spread)


def draw_src_scale(key, part):
    scales = row_scales(jax.random.fold_in(key, 23), S_ROWS)
    source_pick, target_pick = drawn(key)
    source_level, target_level, extra_rows = drawn_scales(key)
    return scales.at[source_pick].set(source_level)


def draw_tgt_scale(key, part):
    scales = row_scales(jax.random.fold_in(key, 24), T_ROWS)
    source_pick, target_pick = drawn(key)
    source_level, target_level, extra_rows = drawn_scales(key)
    scales = scales.at[extra_rows].set(3.0)
    return scales.at[target_pick].set(target_level)


def ragged_counts(key, blocks, per_block):
    counts = jax.random.randint(jax.random.fold_in(key, 1), (blocks,), per_block // 2, per_block + 1)
    full_block = jax.random.randint(jax.random.fold_in(key, 2), (), 0, blocks)
    return counts.at[full_block].set(per_block).astype(jnp.int32)


def draw_src_count(key, part):
    return ragged_counts(jax.random.fold_in(key, 31), S_ROWS // S_DEV, S_DEV)


def draw_tgt_count(key, part):
    return ragged_counts(jax.random.fold_in(key, 32), T_ROWS // T_DEV, T_DEV)


def setup_inputs(seed: int = 0, part: int = 0) -> dict:
    key_list = jax.random.split(jax.random.key(seed), 7)
    part_splits = jax.random.split(jax.random.fold_in(key_list[6], part), 7)
    src_emb = draw_src_emb(jax.random.fold_in(jax.random.fold_in(key_list[6], part), 71), part)
    src_scale = draw_src_scale(jax.random.fold_in(jax.random.fold_in(key_list[6], part), 71), part)
    src_count = draw_src_count(jax.random.fold_in(jax.random.fold_in(key_list[6], part), 71), part)
    tgt_emb = draw_tgt_emb(jax.random.fold_in(jax.random.fold_in(key_list[6], part), 71), part)
    tgt_scale = draw_tgt_scale(jax.random.fold_in(jax.random.fold_in(key_list[6], part), 71), part)
    tgt_count = draw_tgt_count(jax.random.fold_in(jax.random.fold_in(key_list[6], part), 71), part)
    return dict(src_emb=src_emb, src_scale=src_scale, src_count=src_count, tgt_emb=tgt_emb, tgt_scale=tgt_scale, tgt_count=tgt_count)


NEG_BIG = -1.0e30


def reference(src_emb, src_scale, src_count, tgt_emb, tgt_scale, tgt_count):
    src_live = (jnp.arange(S_DEV, dtype=jnp.int32)[None, :] < src_count[:, None]).reshape(-1)
    tgt_live = (jnp.arange(T_DEV, dtype=jnp.int32)[None, :] < tgt_count[:, None]).reshape(-1)
    step_rows = math.gcd(S_ROWS, 512)
    blocks = S_ROWS // step_rows
    inputs = (src_emb.reshape(blocks, step_rows, D), src_scale.reshape(blocks, step_rows), src_live.reshape(blocks, step_rows))

    def scores_of(rows_in, scales_in):
        product = jnp.dot(rows_in, tgt_emb.T, preferred_element_type=jnp.float32)
        return product * tgt_scale[None, :] * scales_in[:, None]

    def first_step(totals, blocked):
        col_max, col_sum = totals
        rows_in, scales_in, alive = blocked
        scores = scores_of(rows_in, scales_in)
        row_max = jnp.max(jnp.where(tgt_live[None, :], scores, NEG_BIG), axis=1)
        row_sum = jnp.sum(jnp.where(tgt_live[None, :], jnp.exp(scores - row_max[:, None]), 0.0), axis=1)
        part_max = jnp.max(jnp.where(alive[:, None], scores, NEG_BIG), axis=0)
        part_sum = jnp.sum(jnp.where(alive[:, None], jnp.exp(scores - part_max[None, :]), 0.0), axis=0)
        highest = jnp.maximum(col_max, part_max)
        merged = col_sum * jnp.exp(col_max - highest) + part_sum * jnp.exp(part_max - highest)
        return (highest, merged), row_max + jnp.log(row_sum)

    start_first = (jnp.full((T_ROWS,), NEG_BIG, jnp.float32), jnp.zeros((T_ROWS,), jnp.float32))
    (col_max, col_sum), row_den = lax.scan(first_step, start_first, inputs)
    col_den = jnp.where(tgt_live, col_max + jnp.log(jnp.where(tgt_live, col_sum, 1.0)), 0.0)

    def second_step(col_best, blocked):
        rows_in, scales_in, alive, den_rows = blocked
        scores = scores_of(rows_in, scales_in)
        margin = scores - 0.5 * (den_rows[:, None] + col_den[None, :])
        row_best = jnp.max(jnp.where(tgt_live[None, :], margin, NEG_BIG), axis=1)
        part_best = jnp.max(jnp.where(alive[:, None], margin, NEG_BIG), axis=0)
        return jnp.maximum(col_best, part_best), row_best

    col_best, row_best = lax.scan(second_step, jnp.full((T_ROWS,), NEG_BIG, jnp.float32), inputs + (row_den,))
    best_source = jnp.where(src_live, row_best.reshape(-1), 0.0)
    best_target = jnp.where(tgt_live, col_best, 0.0)
    return (best_source, best_target)
```

```python
import functools

import jax
import jax.numpy as jnp
from jax import lax
from jax.experimental import pallas as pl
from jax.experimental.pallas import tpu as pltpu
from jax.sharding import PartitionSpec as P

NEG_BIG = -1e30
LANES = 128
VMEM = pl.BlockSpec(memory_space=pltpu.VMEM)
SMEM = pl.BlockSpec(memory_space=pltpu.SMEM)


def exchange_masks(ranks):
    bits = ranks.bit_length() - 1
    return [(1 << k) | 1 for k in range(bits - 1, 0, -1)] + [1]


def slot_of(masks, offset):
    bits = len(masks)
    slot = 0
    parity = offset & 1
    for step in range(bits - 1):
        bit = (offset >> (bits - 1 - step)) & 1
        parity = parity ^ bit
        slot = slot + bit * (1 << step)
    return slot + parity * (1 << (bits - 1))


def packed_targets(tgt_emb, tgt_scale, tgt_count):
    rows = tgt_emb.shape[0]
    live = jnp.arange(rows, dtype=jnp.int32) < tgt_count[0]
    scale = jnp.where(live, tgt_scale, 0.0)
    high = lax.reduce_precision(scale, 8, 7)
    middle = lax.reduce_precision(scale - high, 8, 7)
    low = (scale - high) - middle
    lane = jnp.arange(LANES, dtype=jnp.int32)[None, :]
    terms = jnp.where(
        lane == 0, high[:, None], jnp.where(lane == 1, middle[:, None], jnp.where(lane == 2, low[:, None], 0.0))
    )
    return jnp.concatenate([tgt_emb, terms.astype(jnp.bfloat16)], axis=1)


def diagonal():
    shape = (LANES, LANES)
    return lax.broadcasted_iota(jnp.int32, shape, 0) == lax.broadcasted_iota(jnp.int32, shape, 1)


def column_to_row(column, eye):
    return jnp.sum(jnp.where(eye, column, 0.0), axis=0, keepdims=True)


def row_to_column(row, eye):
    return jnp.sum(jnp.where(eye, row, 0.0), axis=1, keepdims=True)


def score_kernel(
    masks, tgt_dev, count_ref, near_ref, far_ref, src_ref, src_scale_ref,
    scores_ref, row_den_ref, stats_ref, tgt_sc,
):
    ranks = 1 << len(masks)
    me = lax.axis_index("blk")
    total, width = tgt_sc.shape
    depth = src_ref.shape[1]
    sources = src_ref.shape[0]
    half = near_ref.shape[0]
    for owner in range(ranks):
        slot = slot_of(masks, me ^ owner)
        rows = pl.ds(owner * tgt_dev, tgt_dev)
        inner = slot & (ranks // 2 - 1)
        at = pl.ds(pl.multiple_of(inner * tgt_dev, tgt_dev), tgt_dev)

        @pl.when(slot < ranks // 2)
        def _():
            tgt_sc[rows, :] = near_ref[at, :]

        @pl.when(slot >= ranks // 2)
        def _():
            tgt_sc[rows, :] = far_ref[at, :]

    src_live = lax.broadcasted_iota(jnp.int32, (1, sources), 1) < count_ref[0]
    src_scale = src_scale_ref[...]
    eye = diagonal()
    blocks = total // LANES
    row_max = jnp.full((1, sources), NEG_BIG, jnp.float32)
    for block in range(blocks):
        rows = pl.ds(block * LANES, LANES)
        product = lax.dot_general(
            tgt_sc[rows, :depth], src_ref[...], (((1,), (1,)), ((), ())), preferred_element_type=jnp.float32
        )
        scale = jnp.sum(tgt_sc[rows, depth:].astype(jnp.float32), axis=1, keepdims=True)
        scores = jnp.where(scale > 0.0, product * scale * src_scale, NEG_BIG)
        scores_ref[rows, :] = scores
        row_max = jnp.maximum(row_max, jnp.max(scores, axis=0, keepdims=True))
        masked = jnp.where(src_live, scores, NEG_BIG)
        highest = jnp.max(masked, axis=1, keepdims=True)
        part = jnp.sum(jnp.exp(masked - highest), axis=1, keepdims=True)
        stats_ref[0, pl.ds(block, 1), :] = column_to_row(highest + jnp.log(part), eye)
    row_sum = jnp.zeros((1, sources), jnp.float32)
    for block in range(blocks):
        rows = pl.ds(block * LANES, LANES)
        row_sum = row_sum + jnp.sum(jnp.exp(scores_ref[rows, :] - row_max), axis=0, keepdims=True)
    row_den = row_max + jnp.log(row_sum)
    row_den_ref[...] = row_den
    half_den = 0.5 * row_den
    for block in range(blocks):
        rows = pl.ds(block * LANES, LANES)
        partial = jnp.where(src_live, scores_ref[rows, :] - half_den, NEG_BIG)
        stats_ref[0, pl.ds(blocks + block, 1), :] = column_to_row(jnp.max(partial, axis=1, keepdims=True), eye)
    pad = stats_ref.shape[1] - 2 * blocks
    if pad:
        stats_ref[0, pl.ds(2 * blocks, pad), :] = jnp.zeros((pad, LANES), jnp.float32)
    for peer in range(1, ranks):
        stats_ref[peer] = stats_ref[0]


def finish_kernel(
    tgt_dev, count_ref, tgt_count_ref, stats_ref, scores_ref, row_den_ref, best_source_ref, best_target_ref
):
    me = lax.axis_index("blk")
    total, sources = scores_ref.shape
    blocks = total // LANES
    eye = diagonal()
    logs = stats_ref[:, :blocks, :]
    highest = jnp.max(logs, axis=0)
    col_den = highest + jnp.log(jnp.sum(jnp.exp(logs - highest[None]), axis=0))
    best = jnp.max(stats_ref[:, blocks : 2 * blocks, :], axis=0) - 0.5 * col_den
    row_best = jnp.full((1, sources), NEG_BIG, jnp.float32)
    for block in range(blocks):
        half_den = row_to_column(0.5 * col_den[block : block + 1, :], eye)
        rows = pl.ds(block * LANES, LANES)
        scores = scores_ref[rows, :]
        margin = jnp.where(scores > 0.5 * NEG_BIG, scores - half_den, NEG_BIG)
        row_best = jnp.maximum(row_best, jnp.max(margin, axis=0, keepdims=True))
    src_live = lax.broadcasted_iota(jnp.int32, (1, sources), 1) < count_ref[0]
    best_source_ref[...] = jnp.where(src_live, row_best - 0.5 * row_den_ref[...], 0.0)
    lane = lax.broadcasted_iota(jnp.int32, (tgt_dev, LANES), 1)
    wanted = lax.broadcasted_iota(jnp.int32, (tgt_dev, LANES), 0) + me * tgt_dev
    own = jnp.zeros((tgt_dev, 1), jnp.float32)
    for block in range(blocks):
        hit = lane + block * LANES == wanted
        own = own + jnp.sum(jnp.where(hit, best[block : block + 1, :], 0.0), axis=1, keepdims=True)
    line = (tgt_dev, tgt_dev)
    same = lax.broadcasted_iota(jnp.int32, line, 0) == lax.broadcasted_iota(jnp.int32, line, 1)
    own = jnp.sum(jnp.where(same, own, 0.0), axis=0, keepdims=True)
    own_live = lax.broadcasted_iota(jnp.int32, (1, tgt_dev), 1) < tgt_count_ref[0]
    best_target_ref[...] = jnp.where(own_live, own, 0.0)


def body(src_emb, src_scale, src_count, tgt_emb, tgt_scale, tgt_count):
    ranks = lax.axis_size("blk")
    src_dev, depth = src_emb.shape
    tgt_dev = tgt_emb.shape[0]
    total = ranks * tgt_dev
    masks = exchange_masks(ranks)
    held = packed_targets(tgt_emb, tgt_scale, tgt_count)
    for mask in masks[:-1]:
        came = lax.ppermute(held, "blk", [(i, i ^ mask) for i in range(ranks)])
        held = jnp.concatenate([held, came], axis=0)
    far = lax.ppermute(held, "blk", [(i, i ^ masks[-1]) for i in range(ranks)])
    stat_rows = -(-2 * total // (8 * LANES)) * 8
    scores, row_den, stats = pl.pallas_call(
        functools.partial(score_kernel, masks, tgt_dev),
        out_shape=(
            jax.ShapeDtypeStruct((total, src_dev), jnp.float32),
            jax.ShapeDtypeStruct((1, src_dev), jnp.float32),
            jax.ShapeDtypeStruct((ranks, stat_rows, LANES), jnp.float32),
        ),
        in_specs=[SMEM, VMEM, VMEM, VMEM, VMEM],
        out_specs=(VMEM, VMEM, VMEM),
        scratch_shapes=[pltpu.VMEM((total, depth + LANES), jnp.bfloat16)],
        name="scores",
    )(src_count, held, far, src_emb, src_scale.reshape(1, src_dev))
    stats = lax.all_to_all(stats, "blk", split_axis=0, concat_axis=0, tiled=True)
    best_source, best_target = pl.pallas_call(
        functools.partial(finish_kernel, tgt_dev),
        out_shape=(
            jax.ShapeDtypeStruct((1, src_dev), jnp.float32),
            jax.ShapeDtypeStruct((1, tgt_dev), jnp.float32),
        ),
        in_specs=[SMEM, SMEM, VMEM, VMEM, VMEM],
        out_specs=(VMEM, VMEM),
        name="finish",
    )(src_count, tgt_count, stats, scores, row_den)
    return best_source.reshape(src_dev), best_target.reshape(tgt_dev)


def solution(mesh):
    return jax.shard_map(
        body,
        mesh=mesh,
        in_specs=(
            P(("pairs", "blk"), None),
            P(("pairs", "blk")),
            P(("pairs", "blk")),
            P(("pairs", "blk"), None),
            P(("pairs", "blk")),
            P(("pairs", "blk")),
        ),
        out_specs=(P(("pairs", "blk")), P(("pairs", "blk"))),
        check_vma=False,
    )
```

```python
import functools

import jax
import jax.numpy as jnp
from jax import lax
from jax.experimental import pallas as pl
from jax.experimental.pallas import tpu as pltpu
from jax.sharding import PartitionSpec as P


NEG_BIG = -1e30
LANES = 128
VMEM = pl.BlockSpec(memory_space=pltpu.VMEM)
SMEM = pl.BlockSpec(memory_space=pltpu.SMEM)
HBM = pl.BlockSpec(memory_space=pltpu.HBM)


def exchange_phases(ranks):
    bits = list(range(ranks.bit_length() - 2, 0, -1))
    phases = []
    if len(bits) % 2:
        phases.append([(1 << bits.pop(0)) | 1])
    for high, low in zip(bits[::2], bits[1::2]):
        phases.append([(1 << high) | (1 << low) | 1, (1 << high) | 1, (1 << low) | 1])
    return phases


def exchange(block, ranks, mask):
    return lax.ppermute(block, "blk", [(i, i ^ mask) for i in range(ranks)])


def on_chip(array):
    return pltpu.with_memory_space_constraint(array, pltpu.VMEM)


def in_hbm(array):
    return pltpu.with_memory_space_constraint(array, pltpu.HBM)


def diagonal(size):
    shape = (size, size)
    return lax.broadcasted_iota(jnp.int32, shape, 0) == lax.broadcasted_iota(jnp.int32, shape, 1)


def column_to_row(column, eye):
    return jnp.sum(jnp.where(eye, column, 0.0), axis=0, keepdims=True)


def row_to_column(row, eye):
    return jnp.sum(jnp.where(eye, row, 0.0), axis=1, keepdims=True)


def pack_kernel(count_ref, tgt_hbm, scale_hbm, packed_ref, live_ref, scale_ref, sems):
    rows, depth = tgt_hbm.shape
    copies = [
        pltpu.make_async_copy(scale_hbm, scale_ref, sems.at[0]),
        pltpu.make_async_copy(tgt_hbm, packed_ref.at[:, pl.ds(0, depth)], sems.at[1]),
    ]
    for copy in copies:
        copy.start()
    copies[0].wait()
    live = lax.broadcasted_iota(jnp.int32, (1, rows), 1) < count_ref[0]
    live_ref[...] = jnp.where(live, 1.0, 0.0)
    scale = row_to_column(jnp.where(live, scale_ref[...], 0.0), diagonal(rows))
    high = scale.astype(jnp.bfloat16).astype(jnp.float32)
    rest = scale - high
    middle = rest.astype(jnp.bfloat16).astype(jnp.float32)
    low = rest - middle
    lane = lax.broadcasted_iota(jnp.int32, (rows, LANES), 1)
    terms = jnp.where(lane == 0, high, jnp.where(lane == 1, middle, jnp.where(lane == 2, low, 0.0)))
    packed_ref[:, depth:] = terms.astype(jnp.bfloat16)
    copies[1].wait()


def load_kernel(src_hbm, scale_hbm, src_ref, scale_ref, sems):
    copies = [
        pltpu.make_async_copy(src_hbm, src_ref, sems.at[0]),
        pltpu.make_async_copy(scale_hbm, scale_ref, sems.at[1]),
    ]
    for copy in copies:
        copy.start()
    for copy in copies:
        copy.wait()


def half_scores(offsets, blocks_ref, tgt_sc, src_ref, src_scale_ref, src_live, scores_ref, tgt_dev):
    me = lax.axis_index("blk")
    depth = src_ref.shape[1]
    half = tgt_sc.shape[0]
    for slot, offset in enumerate(offsets):
        at = pl.multiple_of(((me ^ offset) >> 1) * tgt_dev, tgt_dev)
        tgt_sc[pl.ds(at, tgt_dev), :] = blocks_ref[pl.ds(slot * tgt_dev, tgt_dev), :]
    eye = diagonal(LANES)
    logs = []
    row_max = jnp.full(src_scale_ref.shape, NEG_BIG, jnp.float32)
    for start in range(0, half, LANES):
        rows = pl.ds(start, LANES)
        product = lax.dot_general(
            tgt_sc[rows, :depth], src_ref[...], (((1,), (1,)), ((), ())), preferred_element_type=jnp.float32
        )
        scale = jnp.sum(tgt_sc[rows, depth:].astype(jnp.float32), axis=1, keepdims=True)
        scores = jnp.where(scale > 0.0, product * scale * src_scale_ref[...], NEG_BIG)
        scores_ref[rows, :] = scores
        row_max = jnp.maximum(row_max, jnp.max(scores, axis=0, keepdims=True))
        masked = jnp.where(src_live, scores, NEG_BIG)
        highest = jnp.max(masked, axis=1, keepdims=True)
        part = jnp.sum(jnp.exp(masked - highest), axis=1, keepdims=True)
        logs.append(column_to_row(highest + jnp.log(part), eye))
    return row_max, logs


def exp_sums(scores_ref, row_max):
    row_sum = jnp.zeros_like(row_max)
    for start in range(0, scores_ref.shape[0], LANES):
        row_sum = row_sum + jnp.sum(jnp.exp(scores_ref[pl.ds(start, LANES), :] - row_max), axis=0, keepdims=True)
    return row_sum


def live_lanes(count_ref, size):
    return lax.broadcasted_iota(jnp.int32, (1, size), 1) < count_ref[0]


def near_kernel(
    offsets, tgt_dev, count_ref, near_ref, src_ref, src_scale_ref, scores_ref, row_max_ref, row_sum_ref, logs_ref, tgt_sc
):
    src_live = live_lanes(count_ref, src_ref.shape[0])
    row_max, logs = half_scores(offsets, near_ref, tgt_sc, src_ref, src_scale_ref, src_live, scores_ref, tgt_dev)
    row_max_ref[...] = row_max
    row_sum_ref[...] = exp_sums(scores_ref, row_max)
    for row, values in enumerate(logs):
        logs_ref[pl.ds(row, 1), :] = values


def near_holds_core_0(phases, tgt_dev, row):
    me = lax.axis_index("blk")
    lane = lax.broadcasted_iota(jnp.int32, (1, LANES), 1) + row * LANES
    away = (lane // tgt_dev) ^ (me >> 1)
    core = jnp.full((1, LANES), me & 1, jnp.int32)
    for masks in phases:
        bits = functools.reduce(lambda a, b: a | b, masks) >> 1
        core = core ^ jnp.where((away & bits) != 0, 1, 0)
    return core == 0


def far_kernel(
    phases, offsets, tgt_dev,
    count_ref, far_ref, src_ref, src_scale_ref, near_scores_ref, near_max_ref, near_sum_ref, near_logs_ref,
    scores_ref, row_den_ref, stats_ref, tgt_sc,
):
    src_live = live_lanes(count_ref, src_ref.shape[0])
    offsets = [offset ^ 1 for offset in offsets]
    far_max, logs = half_scores(offsets, far_ref, tgt_sc, src_ref, src_scale_ref, src_live, scores_ref, tgt_dev)
    row_max = jnp.maximum(near_max_ref[...], far_max)
    row_sum = near_sum_ref[...] * jnp.exp(near_max_ref[...] - row_max) + exp_sums(scores_ref, row_max)
    row_den = row_max + jnp.log(row_sum)
    row_den_ref[...] = row_den
    half_den = 0.5 * row_den
    count = len(logs)
    eye = diagonal(LANES)

    def best(ref, row):
        margin = jnp.where(src_live, ref[pl.ds(row * LANES, LANES), :] - half_den, NEG_BIG)
        return column_to_row(jnp.max(margin, axis=1, keepdims=True), eye)

    for row in range(count):
        near_first = near_holds_core_0(phases, tgt_dev, row)
        pairs = ((near_logs_ref[pl.ds(row, 1), :], logs[row]), (best(near_scores_ref, row), best(scores_ref, row)))
        for kind, (near, far) in enumerate(pairs):
            stats_ref[0, pl.ds((2 * kind) * count + row, 1), :] = jnp.where(near_first, near, far)
            stats_ref[0, pl.ds((2 * kind + 1) * count + row, 1), :] = jnp.where(near_first, far, near)
    for peer in range(1, stats_ref.shape[0]):
        stats_ref[peer] = stats_ref[0]


def finish_kernel(
    phases, tgt_dev, count_ref, own_live_ref, stats_ref, near_ref, far_ref, half_den_ref,
    best_source_ref, best_target_ref,
):
    me = lax.axis_index("blk")
    sources = near_ref.shape[1]
    count = near_ref.shape[0] // LANES
    eye = diagonal(LANES)
    logs = stats_ref[:, : 2 * count, :]
    highest = jnp.max(logs, axis=0)
    half_col = 0.5 * (highest + jnp.log(jnp.sum(jnp.exp(logs - highest[None]), axis=0)))
    best = jnp.max(stats_ref[:, 2 * count :, :], axis=0) - half_col
    row_best = jnp.full((1, sources), NEG_BIG, jnp.float32)
    for row in range(count):
        near_first = near_holds_core_0(phases, tgt_dev, row)
        first, second = half_col[row : row + 1, :], half_col[count + row : count + row + 1, :]
        for ref, values in (
            (near_ref, jnp.where(near_first, first, second)),
            (far_ref, jnp.where(near_first, second, first)),
        ):
            scores = ref[pl.ds(row * LANES, LANES), :]
            margin = jnp.where(scores > 0.5 * NEG_BIG, scores - row_to_column(values, eye), NEG_BIG)
            row_best = jnp.maximum(row_best, jnp.max(margin, axis=0, keepdims=True))
    best_source_ref[...] = jnp.where(live_lanes(count_ref, sources), row_best - half_den_ref[...], 0.0)
    lane = lax.broadcasted_iota(jnp.int32, (tgt_dev, LANES), 1)
    wanted = lax.broadcasted_iota(jnp.int32, (tgt_dev, LANES), 0) + (me >> 1) * tgt_dev
    own = jnp.zeros((tgt_dev, 1), jnp.float32)
    for row in range(count):
        values = jnp.where((me & 1) == 0, best[row : row + 1, :], best[count + row : count + row + 1, :])
        own = own + jnp.sum(jnp.where(lane + row * LANES == wanted, values, 0.0), axis=1, keepdims=True)
    best_target_ref[...] = jnp.where(own_live_ref[...] > 0.5, column_to_row(own, diagonal(tgt_dev)), 0.0)


def mine(src_emb, src_scale, src_count, tgt_emb, tgt_scale, tgt_count):
    ranks = lax.axis_size("blk")
    params = pltpu.CompilerParams(vmem_limit_bytes=24 << 20)
    src_dev, depth = src_emb.shape
    tgt_dev = tgt_emb.shape[0]
    half = ranks // 2 * tgt_dev
    width = depth + LANES
    phases = exchange_phases(ranks)
    source_line = pltpu.VMEM((1, src_dev), jnp.float32)
    half_shape = pltpu.VMEM((half, src_dev), jnp.float32)
    near, own_live = pl.pallas_call(
        pack_kernel,
        out_shape=(pltpu.VMEM((tgt_dev, width), jnp.bfloat16), pltpu.VMEM((1, tgt_dev), jnp.float32)),
        in_specs=[SMEM, HBM, HBM],
        out_specs=(VMEM, VMEM),
        scratch_shapes=[
            pltpu.VMEM((1, tgt_dev), jnp.float32),
            pltpu.SemaphoreType.DMA((2,)),
        ],
        compiler_params=params,
        name="pack",
    )(tgt_count, in_hbm(tgt_emb), in_hbm(tgt_scale.reshape(1, tgt_dev)))
    load = pl.pallas_call(
        load_kernel,
        out_shape=(pltpu.VMEM((src_dev, depth), src_emb.dtype), source_line),
        in_specs=[HBM, HBM],
        out_specs=(VMEM, VMEM),
        scratch_shapes=[pltpu.SemaphoreType.DMA((2,))],
        compiler_params=params,
        cost_estimate=pl.CostEstimate(flops=0, bytes_accessed=2 * src_emb.size * 2, transcendentals=0),
        name="load",
    )
    sources, source_scales = load(in_hbm(src_emb), in_hbm(src_scale.reshape(1, src_dev)))
    offsets = [0]
    for masks in phases:
        came = [exchange(near, ranks, mask) for mask in masks]
        near = jnp.concatenate([near] + came, axis=0)
        offsets = offsets + [offset ^ mask for mask in masks for offset in offsets]
    far = exchange(near, ranks, 1)
    near_scores, near_max, near_sum, near_logs = pl.pallas_call(
        functools.partial(near_kernel, offsets, tgt_dev),
        out_shape=(half_shape, source_line, source_line, pltpu.VMEM((half // LANES, LANES), jnp.float32)),
        in_specs=[SMEM, VMEM, VMEM, VMEM],
        out_specs=(VMEM,) * 4,
        scratch_shapes=[pltpu.VMEM((half, width), jnp.bfloat16)],
        compiler_params=params,
        cost_estimate=pl.CostEstimate(
            flops=2 * half * src_dev * depth, bytes_accessed=4 * half * src_dev, transcendentals=2 * half * src_dev
        ),
        name="near",
    )(src_count, on_chip(near), on_chip(sources), on_chip(source_scales))
    far_scores, row_den, stats = pl.pallas_call(
        functools.partial(far_kernel, phases, offsets, tgt_dev),
        out_shape=(half_shape, source_line, jax.ShapeDtypeStruct((ranks, 4 * half // LANES, LANES), jnp.float32)),
        in_specs=[SMEM] + [VMEM] * 7,
        out_specs=(VMEM,) * 3,
        scratch_shapes=[pltpu.VMEM((half, width), jnp.bfloat16)],
        compiler_params=params,
        name="far",
    )(
        src_count, on_chip(far), on_chip(sources), on_chip(source_scales),
        on_chip(near_scores), on_chip(near_max), on_chip(near_sum), on_chip(near_logs),
    )
    stats = lax.all_to_all(stats, "blk", split_axis=0, concat_axis=0, tiled=True)
    best_source, best_target = pl.pallas_call(
        functools.partial(finish_kernel, phases, tgt_dev),
        out_shape=(
            jax.ShapeDtypeStruct((1, src_dev), jnp.float32),
            jax.ShapeDtypeStruct((1, tgt_dev), jnp.float32),
        ),
        in_specs=[SMEM] + [VMEM] * 5,
        out_specs=(VMEM, VMEM),
        compiler_params=params,
        name="finish",
    )(src_count, on_chip(own_live), on_chip(stats), on_chip(near_scores), on_chip(far_scores), 0.5 * row_den)
    return best_source.reshape(src_dev), best_target.reshape(tgt_dev)


def solution(mesh):
    return jax.shard_map(
        mine,
        mesh=mesh,
        in_specs=(
            P(("pairs", "blk"), None),
            P(("pairs", "blk")),
            P(("pairs", "blk")),
            P(("pairs", "blk"), None),
            P(("pairs", "blk")),
            P(("pairs", "blk")),
        ),
        out_specs=(P(("pairs", "blk")), P(("pairs", "blk"))),
        check_vma=False,
    )
```

```python
import functools

import jax
import jax.numpy as jnp
from jax import lax
from jax.experimental import pallas as pl
from jax.experimental.pallas import tpu as pltpu
from jax.sharding import PartitionSpec as P


NEG_BIG = -1e30
LANES = 128
SMEM = pl.BlockSpec(memory_space=pltpu.SMEM)
VMEM = pl.BlockSpec(memory_space=pltpu.VMEM)
HBM = pl.BlockSpec(memory_space=pltpu.HBM)


def exchange_phases(ranks):
    bits = list(range(ranks.bit_length() - 2, 0, -1))
    phases = []
    if len(bits) % 2:
        phases.append([(1 << bits.pop(0)) | 1])
    for high, low in zip(bits[::2], bits[1::2]):
        phases.append([(1 << high) | (1 << low) | 1, (1 << high) | 1, (1 << low) | 1])
    return phases


def exchange(block, ranks, mask):
    return lax.ppermute(block, "blk", [(i, i ^ mask) for i in range(ranks)])


def on_chip(array):
    return pltpu.with_memory_space_constraint(array, pltpu.VMEM)


def in_hbm(array):
    return pltpu.with_memory_space_constraint(array, pltpu.HBM)


def diagonal(size):
    shape = (size, size)
    return lax.broadcasted_iota(jnp.int32, shape, 0) == lax.broadcasted_iota(jnp.int32, shape, 1)


def column_to_row(column, eye):
    return jnp.sum(jnp.where(eye, column, 0.0), axis=0, keepdims=True)


def row_to_column(row, eye):
    return jnp.sum(jnp.where(eye, row, 0.0), axis=1, keepdims=True)


def pack_kernel(count_ref, tgt_hbm, scale_hbm, packed_ref, live_ref, scale_ref, sems):
    rows, depth = tgt_hbm.shape
    copies = [
        pltpu.make_async_copy(scale_hbm, scale_ref, sems.at[0]),
        pltpu.make_async_copy(tgt_hbm, packed_ref.at[:, pl.ds(0, depth)], sems.at[1]),
    ]
    for copy in copies:
        copy.start()
    copies[0].wait()
    live = lax.broadcasted_iota(jnp.int32, (1, rows), 1) < count_ref[0]
    live_ref[...] = jnp.where(live, 1.0, 0.0)
    scale = row_to_column(jnp.where(live, scale_ref[...], 0.0), diagonal(rows))
    high = scale.astype(jnp.bfloat16).astype(jnp.float32)
    rest = scale - high
    middle = rest.astype(jnp.bfloat16).astype(jnp.float32)
    low = rest - middle
    lane = lax.broadcasted_iota(jnp.int32, (rows, LANES), 1)
    terms = jnp.where(lane == 0, high, jnp.where(lane == 1, middle, jnp.where(lane == 2, low, 0.0)))
    packed_ref[:, depth:] = terms.astype(jnp.bfloat16)
    copies[1].wait()


def load_kernel(count_ref, src_hbm, scale_hbm, src_ref, scale_ref, live_ref, sems):
    copies = [
        pltpu.make_async_copy(src_hbm, src_ref, sems.at[0]),
        pltpu.make_async_copy(scale_hbm, scale_ref, sems.at[1]),
    ]
    for copy in copies:
        copy.start()
    live = lax.broadcasted_iota(jnp.int32, live_ref.shape, 1) < count_ref[0]
    live_ref[...] = jnp.where(live, 1.0, 0.0)
    for copy in copies:
        copy.wait()


def half_scores(offsets, blocks_ref, tgt_sc, src_ref, src_scale_ref, src_live, scores_ref, tgt_dev):
    me = lax.axis_index("blk")
    depth = src_ref.shape[1]
    half = tgt_sc.shape[0]
    for slot, offset in enumerate(offsets):
        at = pl.multiple_of(((me ^ offset) >> 1) * tgt_dev, tgt_dev)
        tgt_sc[pl.ds(at, tgt_dev), :] = blocks_ref[pl.ds(slot * tgt_dev, tgt_dev), :]
    eye = diagonal(LANES)
    logs = []
    row_max = jnp.full(src_scale_ref.shape, NEG_BIG, jnp.float32)
    for start in range(0, half, LANES):
        rows = pl.ds(start, LANES)
        product = lax.dot_general(
            tgt_sc[rows, :depth], src_ref[...], (((1,), (1,)), ((), ())), preferred_element_type=jnp.float32
        )
        scale = jnp.sum(tgt_sc[rows, depth:].astype(jnp.float32), axis=1, keepdims=True)
        scores = jnp.where(scale > 0.0, product * scale * src_scale_ref[...], NEG_BIG)
        scores_ref[rows, :] = scores
        row_max = jnp.maximum(row_max, jnp.max(scores, axis=0, keepdims=True))
        masked = jnp.where(src_live, scores, NEG_BIG)
        highest = jnp.max(masked, axis=1, keepdims=True)
        part = jnp.sum(jnp.exp(masked - highest), axis=1, keepdims=True)
        logs.append(column_to_row(highest + jnp.log(part), eye))
    return row_max, logs


def exp_sums(scores_ref, row_max):
    row_sum = jnp.zeros_like(row_max)
    for start in range(0, scores_ref.shape[0], LANES):
        row_sum = row_sum + jnp.sum(jnp.exp(scores_ref[pl.ds(start, LANES), :] - row_max), axis=0, keepdims=True)
    return row_sum


def near_kernel(
    offsets, tgt_dev, src_live_ref, near_ref, src_ref, src_scale_ref, scores_ref, row_max_ref, row_sum_ref, logs_ref, tgt_sc
):
    src_live = src_live_ref[...] > 0.5
    row_max, logs = half_scores(offsets, near_ref, tgt_sc, src_ref, src_scale_ref, src_live, scores_ref, tgt_dev)
    row_max_ref[...] = row_max
    row_sum_ref[...] = exp_sums(scores_ref, row_max)
    for row, values in enumerate(logs):
        logs_ref[pl.ds(row, 1), :] = values


def near_holds_core_0(phases, tgt_dev, row):
    me = lax.axis_index("blk")
    lane = lax.broadcasted_iota(jnp.int32, (1, LANES), 1) + row * LANES
    away = (lane // tgt_dev) ^ (me >> 1)
    core = jnp.full((1, LANES), me & 1, jnp.int32)
    for masks in phases:
        bits = functools.reduce(lambda a, b: a | b, masks) >> 1
        core = core ^ jnp.where((away & bits) != 0, 1, 0)
    return core == 0


def far_kernel(
    phases, offsets, tgt_dev,
    src_live_ref, far_ref, src_ref, src_scale_ref, near_scores_ref, near_max_ref, near_sum_ref, near_logs_ref,
    scores_ref, row_den_ref, stats_ref, tgt_sc,
):
    src_live = src_live_ref[...] > 0.5
    offsets = [offset ^ 1 for offset in offsets]
    far_max, logs = half_scores(offsets, far_ref, tgt_sc, src_ref, src_scale_ref, src_live, scores_ref, tgt_dev)
    row_max = jnp.maximum(near_max_ref[...], far_max)
    row_sum = near_sum_ref[...] * jnp.exp(near_max_ref[...] - row_max) + exp_sums(scores_ref, row_max)
    row_den = row_max + jnp.log(row_sum)
    row_den_ref[...] = row_den
    half_den = 0.5 * row_den
    count = len(logs)
    eye = diagonal(LANES)

    def best(ref, row):
        margin = jnp.where(src_live, ref[pl.ds(row * LANES, LANES), :] - half_den, NEG_BIG)
        return column_to_row(jnp.max(margin, axis=1, keepdims=True), eye)

    for row in range(count):
        near_first = near_holds_core_0(phases, tgt_dev, row)
        pairs = ((near_logs_ref[pl.ds(row, 1), :], logs[row]), (best(near_scores_ref, row), best(scores_ref, row)))
        for kind, (near, far) in enumerate(pairs):
            stats_ref[pl.ds((2 * kind) * count + row, 1), :] = jnp.where(near_first, near, far)
            stats_ref[pl.ds((2 * kind + 1) * count + row, 1), :] = jnp.where(near_first, far, near)


def merged(parts):
    highest = functools.reduce(jnp.maximum, parts)
    logs = highest + jnp.log(sum(jnp.exp(part - highest) for part in parts))
    row = lax.broadcasted_iota(jnp.int32, highest.shape, 0)
    return jnp.where(row < highest.shape[0] // 2, logs, highest)


def finish_kernel(
    phases, tgt_dev, src_live_ref, own_live_ref, stats_ref, near_ref, far_ref, row_den_ref,
    best_source_ref, best_target_ref,
):
    me = lax.axis_index("blk")
    sources = near_ref.shape[1]
    count = near_ref.shape[0] // LANES
    eye = diagonal(LANES)
    half_col = 0.5 * stats_ref[: 2 * count, :]
    best = stats_ref[2 * count :, :] - half_col
    row_best = jnp.full((1, sources), NEG_BIG, jnp.float32)
    for row in range(count):
        near_first = near_holds_core_0(phases, tgt_dev, row)
        first, second = half_col[row : row + 1, :], half_col[count + row : count + row + 1, :]
        for ref, values in (
            (near_ref, jnp.where(near_first, first, second)),
            (far_ref, jnp.where(near_first, second, first)),
        ):
            scores = ref[pl.ds(row * LANES, LANES), :]
            margin = jnp.where(scores > 0.5 * NEG_BIG, scores - row_to_column(values, eye), NEG_BIG)
            row_best = jnp.maximum(row_best, jnp.max(margin, axis=0, keepdims=True))
    best_source_ref[...] = jnp.where(src_live_ref[...] > 0.5, row_best - 0.5 * row_den_ref[...], 0.0)
    lane = lax.broadcasted_iota(jnp.int32, (tgt_dev, LANES), 1)
    wanted = lax.broadcasted_iota(jnp.int32, (tgt_dev, LANES), 0) + (me >> 1) * tgt_dev
    own = jnp.zeros((tgt_dev, 1), jnp.float32)
    for row in range(count):
        values = jnp.where((me & 1) == 0, best[row : row + 1, :], best[count + row : count + row + 1, :])
        own = own + jnp.sum(jnp.where(lane + row * LANES == wanted, values, 0.0), axis=1, keepdims=True)
    best_target_ref[...] = jnp.where(own_live_ref[...] > 0.5, column_to_row(own, diagonal(tgt_dev)), 0.0)


def mine(src_emb, src_scale, src_count, tgt_emb, tgt_scale, tgt_count):
    ranks = lax.axis_size("blk")
    params = pltpu.CompilerParams(vmem_limit_bytes=24 << 20)
    src_dev, depth = src_emb.shape
    tgt_dev = tgt_emb.shape[0]
    half = ranks // 2 * tgt_dev
    width = depth + LANES
    phases = exchange_phases(ranks)
    source_line = pltpu.VMEM((1, src_dev), jnp.float32)
    half_shape = pltpu.VMEM((half, src_dev), jnp.float32)
    near, own_live = pl.pallas_call(
        pack_kernel,
        out_shape=(pltpu.VMEM((tgt_dev, width), jnp.bfloat16), pltpu.VMEM((1, tgt_dev), jnp.float32)),
        in_specs=[SMEM, HBM, HBM],
        out_specs=(VMEM, VMEM),
        scratch_shapes=[
            pltpu.VMEM((1, tgt_dev), jnp.float32),
            pltpu.SemaphoreType.DMA((2,)),
        ],
        compiler_params=params,
        name="pack",
    )(tgt_count, in_hbm(tgt_emb), in_hbm(tgt_scale.reshape(1, tgt_dev)))
    load = pl.pallas_call(
        load_kernel,
        out_shape=(pltpu.VMEM((src_dev, depth), src_emb.dtype), source_line, source_line),
        in_specs=[SMEM, HBM, HBM],
        out_specs=(VMEM,) * 3,
        scratch_shapes=[pltpu.SemaphoreType.DMA((2,))],
        compiler_params=params,
        cost_estimate=pl.CostEstimate(flops=0, bytes_accessed=2 * src_emb.size * 2, transcendentals=0),
        name="load",
    )
    sources, source_scales, sources_live = load(
        src_count, in_hbm(src_emb), in_hbm(src_scale.reshape(1, src_dev))
    )
    offsets = [0]
    for masks in phases:
        came = [exchange(near, ranks, mask) for mask in masks]
        near = jnp.concatenate([near] + came, axis=0)
        offsets = offsets + [offset ^ mask for mask in masks for offset in offsets]
    far = exchange(near, ranks, 1)
    near_scores, near_max, near_sum, near_logs = pl.pallas_call(
        functools.partial(near_kernel, offsets, tgt_dev),
        out_shape=(half_shape, source_line, source_line, pltpu.VMEM((half // LANES, LANES), jnp.float32)),
        in_specs=[VMEM] * 4,
        out_specs=(VMEM,) * 4,
        scratch_shapes=[pltpu.VMEM((half, width), jnp.bfloat16)],
        compiler_params=params,
        cost_estimate=pl.CostEstimate(
            flops=2 * half * src_dev * depth, bytes_accessed=4 * half * src_dev, transcendentals=2 * half * src_dev
        ),
        name="near",
    )(on_chip(sources_live), on_chip(near), on_chip(sources), on_chip(source_scales))
    far_scores, row_den, stats = pl.pallas_call(
        functools.partial(far_kernel, phases, offsets, tgt_dev),
        out_shape=(half_shape, source_line, pltpu.VMEM((4 * half // LANES, LANES), jnp.float32)),
        in_specs=[VMEM] * 8,
        out_specs=(VMEM,) * 3,
        scratch_shapes=[pltpu.VMEM((half, width), jnp.bfloat16)],
        compiler_params=params,
        name="far",
    )(
        on_chip(sources_live), on_chip(far), on_chip(sources), on_chip(source_scales),
        on_chip(near_scores), on_chip(near_max), on_chip(near_sum), on_chip(near_logs),
    )
    stats = merged([stats, exchange(stats, ranks, 1)])
    for masks in phases:
        came = [exchange(stats, ranks, mask) for mask in masks]
        stats = merged([stats] + came)
    best_source, best_target = pl.pallas_call(
        functools.partial(finish_kernel, phases, tgt_dev),
        out_shape=(
            jax.ShapeDtypeStruct((1, src_dev), jnp.float32),
            jax.ShapeDtypeStruct((1, tgt_dev), jnp.float32),
        ),
        in_specs=[VMEM] * 6,
        out_specs=(VMEM, VMEM),
        compiler_params=params,
        name="finish",
    )(on_chip(sources_live), on_chip(own_live), on_chip(stats), on_chip(near_scores), on_chip(far_scores), on_chip(row_den))
    return best_source.reshape(src_dev), best_target.reshape(tgt_dev)


def solution(mesh):
    return jax.shard_map(
        mine,
        mesh=mesh,
        in_specs=(
            P(("pairs", "blk"), None),
            P(("pairs", "blk")),
            P(("pairs", "blk")),
            P(("pairs", "blk"), None),
            P(("pairs", "blk")),
            P(("pairs", "blk")),
        ),
        out_specs=(P(("pairs", "blk")), P(("pairs", "blk"))),
        check_vma=False,
    )
```

```python
import functools

import jax
import jax.numpy as jnp
from jax import lax
from jax.experimental import pallas as pl
from jax.experimental.pallas import tpu as pltpu
from jax.sharding import PartitionSpec as P


NEG_BIG = -1e30
LOG2_E = 1.4426950408889634
LN_2 = 0.6931471805599453
LANES = 128
SMEM = pl.BlockSpec(memory_space=pltpu.SMEM)
VMEM = pl.BlockSpec(memory_space=pltpu.VMEM)
HBM = pl.BlockSpec(memory_space=pltpu.HBM)


def exchange_phases(ranks):
    bits = list(range(ranks.bit_length() - 2, 0, -1))
    phases = [[bits.pop(0)]] if len(bits) % 2 else []
    return phases + [[low, high] for high, low in zip(bits[::2], bits[1::2])]


def phase_masks(bits):
    masks = [0]
    for bit in bits:
        masks = masks + [mask | (1 << bit) for mask in masks]
    return [mask | 1 for mask in masks[1:]]


def own_slot(phases, rank):
    place = 0
    for index, bit in enumerate(sum(phases, [])):
        place = place | (((rank >> bit) & 1) << index)
    return place


def crossed(phases, slot):
    crossing, index = 0, 0
    for bits in phases:
        part = (slot >> index) & ((1 << len(bits)) - 1)
        crossing = crossing ^ jnp.where(part != 0, 1, 0)
        index += len(bits)
    return crossing


def exchange(block, ranks, mask):
    return lax.ppermute(block, "blk", [(i, i ^ mask) for i in range(ranks)])


def on_chip(array):
    return pltpu.with_memory_space_constraint(array, pltpu.VMEM)


def in_hbm(array):
    return pltpu.with_memory_space_constraint(array, pltpu.HBM)


def diagonal(size):
    shape = (size, size)
    return lax.broadcasted_iota(jnp.int32, shape, 0) == lax.broadcasted_iota(jnp.int32, shape, 1)


def column_to_row(column, eye):
    return jnp.sum(jnp.where(eye, column, 0.0), axis=0, keepdims=True)


def row_to_column(row, eye):
    return jnp.sum(jnp.where(eye, row, 0.0), axis=1, keepdims=True)


def pack_kernel(count_ref, tgt_hbm, scale_hbm, packed_ref, live_ref, scale_ref, sems):
    rows, depth = tgt_hbm.shape
    copies = [
        pltpu.make_async_copy(scale_hbm, scale_ref, sems.at[0]),
        pltpu.make_async_copy(tgt_hbm, packed_ref.at[:, pl.ds(0, depth)], sems.at[1]),
    ]
    for copy in copies:
        copy.start()
    copies[0].wait()
    live = lax.broadcasted_iota(jnp.int32, (1, rows), 1) < count_ref[0]
    live_ref[...] = jnp.where(live, 1.0, 0.0)
    scale = row_to_column(jnp.where(live, scale_ref[...], 0.0), diagonal(rows))
    high = scale.astype(jnp.bfloat16).astype(jnp.float32)
    rest = scale - high
    middle = rest.astype(jnp.bfloat16).astype(jnp.float32)
    low = rest - middle
    lane = lax.broadcasted_iota(jnp.int32, (rows, LANES), 1)
    terms = jnp.where(lane == 0, high, jnp.where(lane == 1, middle, jnp.where(lane == 2, low, 0.0)))
    packed_ref[:, depth:] = terms.astype(jnp.bfloat16)
    copies[1].wait()


def load_kernel(src_hbm, scale_hbm, src_ref, scale_ref, sems):
    copies = [
        pltpu.make_async_copy(src_hbm, src_ref, sems.at[0]),
        pltpu.make_async_copy(scale_hbm, scale_ref, sems.at[1]),
    ]
    for copy in copies:
        copy.start()
    copies[1].wait()
    scale_ref[...] = scale_ref[...] * LOG2_E
    copies[0].wait()


def column_block(sources):
    return 2 * LANES if sources % (2 * LANES) == 0 else LANES


def fold(values, op):
    return functools.reduce(op, [values[:, at : at + LANES] for at in range(0, values.shape[1], LANES)])


class Half:
    def __init__(self, blocks_ref, src_ref, scale_ref, live_ref, scores_ref, peak_sc, sum_sc):
        self.blocks, self.src, self.scale, self.live = blocks_ref, src_ref, scale_ref, live_ref
        self.scores, self.peak, self.sums = scores_ref, peak_sc, sum_sc
        self.starts = range(0, blocks_ref.shape[0], LANES)

    def columns(self, at, size):
        depth = self.src.shape[1]
        columns = pl.ds(at, size)
        live = self.live[:, columns] > 0.5
        largest = []
        for start in self.starts:
            rows = pl.ds(start, LANES)
            product = lax.dot_general(
                self.blocks[rows, :depth], self.src[columns, :], (((1,), (1,)), ((), ())),
                preferred_element_type=jnp.float32,
            )
            scale = jnp.sum(self.blocks[rows, depth:].astype(jnp.float32), axis=1, keepdims=True)
            scores = jnp.where(scale > 0.0, product * scale * self.scale[:, columns], NEG_BIG)
            self.scores[rows, columns] = scores
            largest.append(jnp.max(scores, axis=0, keepdims=True))
            masked = jnp.where(live, scores, NEG_BIG)
            peak = fold(masked, jnp.maximum)
            if at:
                before = self.peak[rows, :]
                peak = jnp.maximum(before, peak)
            sums = functools.reduce(
                jnp.add, [jnp.exp2(masked[:, tile : tile + LANES] - peak) for tile in range(0, size, LANES)]
            )
            if at:
                sums = sums + self.sums[rows, :] * jnp.exp2(before - peak)
            self.peak[rows, :] = peak
            self.sums[rows, :] = sums
        return functools.reduce(jnp.maximum, largest)

    def exp_sums(self, at, size, row_max):
        columns = pl.ds(at, size)
        parts = [
            jnp.sum(jnp.exp2(self.scores[pl.ds(start, LANES), columns] - row_max), axis=0, keepdims=True)
            for start in self.starts
        ]
        return functools.reduce(jnp.add, parts)

    def logs(self, eye):
        rows = []
        for start in self.starts:
            peak = self.peak[pl.ds(start, LANES), :]
            highest = jnp.max(peak, axis=1, keepdims=True)
            total = jnp.sum(self.sums[pl.ds(start, LANES), :] * jnp.exp2(peak - highest), axis=1, keepdims=True)
            rows.append(column_to_row(highest + jnp.log(total) * LOG2_E, eye))
        return rows


def near_kernel(
    near_ref, src_ref, src_scale_ref, src_live_ref, scores_ref, row_max_ref, row_sum_ref, logs_ref, peak_sc, sum_sc
):
    half = Half(near_ref, src_ref, src_scale_ref, src_live_ref, scores_ref, peak_sc, sum_sc)
    sources = src_ref.shape[0]
    size = column_block(sources)
    for at in range(0, sources, size):
        row_max = half.columns(at, size)
        row_max_ref[:, pl.ds(at, size)] = row_max
        row_sum_ref[:, pl.ds(at, size)] = half.exp_sums(at, size, row_max)
    for row, values in enumerate(half.logs(diagonal(LANES))):
        logs_ref[pl.ds(row, 1), :] = values


def slot_lanes(phases, tgt_dev, row):
    me = lax.axis_index("blk")
    lane = lax.broadcasted_iota(jnp.int32, (1, LANES), 1)
    slot = (lane + row * LANES) // tgt_dev
    core_0 = (crossed(phases, slot) ^ (me & 1)) == 0
    return core_0, lane ^ ((own_slot(phases, me) * tgt_dev) & (LANES - 1))


def shared_row(phases, tgt_dev, row):
    return row ^ ((own_slot(phases, lax.axis_index("blk")) * tgt_dev) // LANES)


def permuted(row, lanes):
    shape = (8, LANES)
    lanes = jnp.broadcast_to(lanes, shape)
    return jnp.take_along_axis(jnp.broadcast_to(row, shape), lanes, axis=1)[:1, :]


def far_kernel(
    phases, tgt_dev,
    far_ref, src_ref, src_scale_ref, src_live_ref, near_scores_ref, near_max_ref, near_sum_ref, near_logs_ref,
    scores_ref, row_den_ref, stats_ref, peak_sc, sum_sc, near_best_sc, far_best_sc,
):
    half = Half(far_ref, src_ref, src_scale_ref, src_live_ref, scores_ref, peak_sc, sum_sc)
    sources = src_ref.shape[0]
    size = column_block(sources)
    for at in range(0, sources, size):
        columns = pl.ds(at, size)
        far_max = half.columns(at, size)
        near_max = near_max_ref[:, columns]
        row_max = jnp.maximum(near_max, far_max)
        row_sum = near_sum_ref[:, columns] * jnp.exp2(near_max - row_max) + half.exp_sums(at, size, row_max)
        row_den = row_max + jnp.log(row_sum) * LOG2_E
        row_den_ref[:, columns] = row_den
        taken = jnp.where(src_live_ref[:, columns] > 0.5, 0.5 * row_den, -NEG_BIG)
        for ref, best_sc in ((near_scores_ref, near_best_sc), (scores_ref, far_best_sc)):
            for start in half.starts:
                rows = pl.ds(start, LANES)
                best = fold(ref[rows, columns] - taken, jnp.maximum)
                best_sc[rows, :] = jnp.maximum(best_sc[rows, :], best) if at else best
    eye = diagonal(LANES)
    count = len(half.starts)
    logs = half.logs(eye)
    for row, start in enumerate(half.starts):
        rows = pl.ds(start, LANES)
        near_best, far_best = (
            column_to_row(jnp.max(best_sc[rows, :], axis=1, keepdims=True), eye)
            for best_sc in (near_best_sc, far_best_sc)
        )
        core_0, lanes = slot_lanes(phases, tgt_dev, row)
        place = shared_row(phases, tgt_dev, row)
        pairs = ((near_logs_ref[pl.ds(row, 1), :], logs[row]), (near_best, far_best))
        for kind, (near, far) in enumerate(pairs):
            for core, values in enumerate((jnp.where(core_0, near, far), jnp.where(core_0, far, near))):
                stats_ref[pl.ds((2 * kind + core) * count + place, 1), :] = permuted(values, lanes)


def merged(parts):
    highest = functools.reduce(jnp.maximum, parts)
    logs = highest + jnp.log(sum(jnp.exp2(part - highest) for part in parts)) * LOG2_E
    row = lax.broadcasted_iota(jnp.int32, highest.shape, 0)
    return jnp.where(row < highest.shape[0] // 2, logs, highest)


def finish_kernel(
    phases, tgt_dev, src_live_ref, own_live_ref, stats_ref, near_ref, far_ref, row_den_ref,
    best_source_ref, best_target_ref,
):
    me = lax.axis_index("blk")
    sources = near_ref.shape[1]
    count = near_ref.shape[0] // LANES
    eye = diagonal(LANES)
    row_best = jnp.full((1, sources), NEG_BIG, jnp.float32)
    for row in range(count):
        core_0, lanes = slot_lanes(phases, tgt_dev, row)
        place = shared_row(phases, tgt_dev, row)
        first = permuted(0.5 * stats_ref[pl.ds(place, 1), :], lanes)
        second = permuted(0.5 * stats_ref[pl.ds(count + place, 1), :], lanes)
        for ref, values in (
            (near_ref, jnp.where(core_0, first, second)),
            (far_ref, jnp.where(core_0, second, first)),
        ):
            margin = ref[pl.ds(row * LANES, LANES), :] - row_to_column(values, eye)
            row_best = jnp.maximum(row_best, jnp.max(margin, axis=0, keepdims=True))
    best_source_ref[...] = jnp.where(src_live_ref[...] > 0.5, (row_best - 0.5 * row_den_ref[...]) * LN_2, 0.0)
    core, first = me & 1, own_slot(phases, me) * tgt_dev
    row = core * count + first // LANES
    best = stats_ref[pl.ds(2 * count + row, 1), :] - 0.5 * stats_ref[pl.ds(row, 1), :]
    lane = lax.broadcasted_iota(jnp.int32, (tgt_dev, LANES), 1)
    wanted = lax.broadcasted_iota(jnp.int32, (tgt_dev, LANES), 0) + (first & (LANES - 1))
    own = jnp.sum(jnp.where(lane == wanted, best * LN_2, 0.0), axis=1, keepdims=True)
    best_target_ref[...] = jnp.where(own_live_ref[...] > 0.5, column_to_row(own, diagonal(tgt_dev)), 0.0)


def mine(src_emb, src_scale, src_count, tgt_emb, tgt_scale, tgt_count):
    ranks = lax.axis_size("blk")
    params = pltpu.CompilerParams(vmem_limit_bytes=24 << 20)
    src_dev, depth = src_emb.shape
    tgt_dev = tgt_emb.shape[0]
    half = ranks // 2 * tgt_dev
    width = depth + LANES
    phases = exchange_phases(ranks)
    source_line = pltpu.VMEM((1, src_dev), jnp.float32)
    half_shape = pltpu.VMEM((half, src_dev), jnp.float32)
    near, own_live = pl.pallas_call(
        pack_kernel,
        out_shape=(pltpu.VMEM((tgt_dev, width), jnp.bfloat16), pltpu.VMEM((1, tgt_dev), jnp.float32)),
        in_specs=[SMEM, HBM, HBM],
        out_specs=(VMEM, VMEM),
        scratch_shapes=[
            pltpu.VMEM((1, tgt_dev), jnp.float32),
            pltpu.SemaphoreType.DMA((2,)),
        ],
        compiler_params=params,
        name="pack",
    )(tgt_count, in_hbm(tgt_emb), in_hbm(tgt_scale.reshape(1, tgt_dev)))
    load = pl.pallas_call(
        load_kernel,
        out_shape=(pltpu.VMEM((src_dev, depth), src_emb.dtype), source_line),
        in_specs=[HBM, HBM],
        out_specs=(VMEM, VMEM),
        scratch_shapes=[pltpu.SemaphoreType.DMA((2,))],
        compiler_params=params,
        cost_estimate=pl.CostEstimate(flops=0, bytes_accessed=2 * src_emb.size * 2, transcendentals=0),
        name="load",
    )
    sources, source_scales = load(in_hbm(src_emb), in_hbm(src_scale.reshape(1, src_dev)))
    sources_live = jnp.where(lax.broadcasted_iota(jnp.int32, (1, src_dev), 1) < src_count, 1.0, 0.0)
    for bits in phases:
        came = [exchange(near, ranks, mask) for mask in phase_masks(bits)]
        near = jnp.concatenate([near] + came, axis=0)
    far = exchange(near, ranks, 1)
    half_lanes = pltpu.VMEM((half, LANES), jnp.float32)
    near_scores, near_max, near_sum, near_logs = pl.pallas_call(
        near_kernel,
        out_shape=(half_shape, source_line, source_line, pltpu.VMEM((half // LANES, LANES), jnp.float32)),
        in_specs=[VMEM] * 4,
        out_specs=(VMEM,) * 4,
        scratch_shapes=[half_lanes] * 2,
        compiler_params=params,
        cost_estimate=pl.CostEstimate(
            flops=2 * half * src_dev * depth, bytes_accessed=4 * half * src_dev, transcendentals=2 * half * src_dev
        ),
        name="near",
    )(on_chip(near), on_chip(sources), on_chip(source_scales), on_chip(sources_live))
    far_scores, row_den, stats = pl.pallas_call(
        functools.partial(far_kernel, phases, tgt_dev),
        out_shape=(half_shape, source_line, pltpu.VMEM((4 * half // LANES, LANES), jnp.float32)),
        in_specs=[VMEM] * 8,
        out_specs=(VMEM,) * 3,
        scratch_shapes=[half_lanes] * 4,
        compiler_params=params,
        name="far",
    )(
        on_chip(far), on_chip(sources), on_chip(source_scales), on_chip(sources_live),
        on_chip(near_scores), on_chip(near_max), on_chip(near_sum), on_chip(near_logs),
    )
    stats = merged([stats, exchange(stats, ranks, 1)])
    for bits in phases:
        came = [exchange(stats, ranks, mask) for mask in phase_masks(bits)]
        stats = merged([stats] + came)
    best_source, best_target = pl.pallas_call(
        functools.partial(finish_kernel, phases, tgt_dev),
        out_shape=(
            jax.ShapeDtypeStruct((1, src_dev), jnp.float32),
            jax.ShapeDtypeStruct((1, tgt_dev), jnp.float32),
        ),
        in_specs=[VMEM] * 6,
        out_specs=(VMEM, VMEM),
        compiler_params=params,
        name="finish",
    )(
        on_chip(sources_live), on_chip(own_live), on_chip(stats), on_chip(near_scores), on_chip(far_scores),
        on_chip(row_den),
    )
    return best_source.reshape(src_dev), best_target.reshape(tgt_dev)


def solution(mesh):
    return jax.shard_map(
        mine,
        mesh=mesh,
        in_specs=(
            P(("pairs", "blk"), None),
            P(("pairs", "blk")),
            P(("pairs", "blk")),
            P(("pairs", "blk"), None),
            P(("pairs", "blk")),
            P(("pairs", "blk")),
        ),
        out_specs=(P(("pairs", "blk")), P(("pairs", "blk"))),
        check_vma=False,
    )
```

```python
import functools

import jax
import jax.numpy as jnp
from jax import lax
from jax.experimental import pallas as pl
from jax.experimental.pallas import tpu as pltpu
from jax.sharding import PartitionSpec as P


NEG_BIG = -1e30
LOG2_E = 1.4426950408889634
LN_2 = 0.6931471805599453
LANES = 128
SMEM = pl.BlockSpec(memory_space=pltpu.SMEM)
VMEM = pl.BlockSpec(memory_space=pltpu.VMEM)
HBM = pl.BlockSpec(memory_space=pltpu.HBM)


def exchange_phases(ranks):
    bits = list(range(ranks.bit_length() - 2, 0, -1))
    phases = [[bits.pop(0)]] if len(bits) % 2 else []
    return phases + [[low, high] for high, low in zip(bits[::2], bits[1::2])]


def phase_masks(bits):
    masks = [0]
    for bit in bits:
        masks = masks + [mask | (1 << bit) for mask in masks]
    return [mask | 1 for mask in masks[1:]]


def own_slot(phases, rank):
    place = 0
    for index, bit in enumerate(sum(phases, [])):
        place = place | (((rank >> bit) & 1) << index)
    return place


def crossed(phases, slot):
    crossing, index = 0, 0
    for bits in phases:
        part = (slot >> index) & ((1 << len(bits)) - 1)
        crossing = crossing ^ jnp.where(part != 0, 1, 0)
        index += len(bits)
    return crossing


def exchange(block, ranks, mask):
    return lax.ppermute(block, "blk", [(i, i ^ mask) for i in range(ranks)])


def on_chip(array):
    return pltpu.with_memory_space_constraint(array, pltpu.VMEM)


def in_hbm(array):
    return pltpu.with_memory_space_constraint(array, pltpu.HBM)


def diagonal(size):
    shape = (size, size)
    return lax.broadcasted_iota(jnp.int32, shape, 0) == lax.broadcasted_iota(jnp.int32, shape, 1)


def column_to_row(column, eye):
    return jnp.sum(jnp.where(eye, column, 0.0), axis=0, keepdims=True)


def row_to_column(row, eye):
    return jnp.sum(jnp.where(eye, row, 0.0), axis=1, keepdims=True)


def pack_kernel(count_ref, tgt_hbm, scale_hbm, packed_ref, live_ref, scale_ref, sems):
    rows, depth = tgt_hbm.shape
    copies = [
        pltpu.make_async_copy(scale_hbm, scale_ref, sems.at[0]),
        pltpu.make_async_copy(tgt_hbm, packed_ref.at[:, pl.ds(0, depth)], sems.at[1]),
    ]
    for copy in copies:
        copy.start()
    copies[0].wait()
    live = lax.broadcasted_iota(jnp.int32, (1, rows), 1) < count_ref[0]
    live_ref[...] = jnp.where(live, 1.0, 0.0)
    scale = row_to_column(jnp.where(live, scale_ref[...], 0.0), diagonal(rows))
    high = scale.astype(jnp.bfloat16).astype(jnp.float32)
    rest = scale - high
    middle = rest.astype(jnp.bfloat16).astype(jnp.float32)
    low = rest - middle
    lane = lax.broadcasted_iota(jnp.int32, (rows, LANES), 1)
    terms = jnp.where(lane == 0, high, jnp.where(lane == 1, middle, jnp.where(lane == 2, low, 0.0)))
    packed_ref[:, depth:] = terms.astype(jnp.bfloat16)
    copies[1].wait()


def load_kernel(src_hbm, scale_hbm, src_ref, scale_ref, sems):
    copies = [
        pltpu.make_async_copy(src_hbm, src_ref, sems.at[0]),
        pltpu.make_async_copy(scale_hbm, scale_ref, sems.at[1]),
    ]
    for copy in copies:
        copy.start()
    copies[1].wait()
    scale_ref[...] = scale_ref[...] * LOG2_E
    copies[0].wait()


def column_block(sources):
    return 4 * LANES if sources % (4 * LANES) == 0 else LANES


def fold(values, op):
    return functools.reduce(op, [values[:, at : at + LANES] for at in range(0, values.shape[1], LANES)])


class Half:
    def __init__(self, blocks_ref, src_ref, scale_ref, live_ref, scores_ref, peak_sc, sum_sc):
        self.blocks, self.src, self.scale, self.live = blocks_ref, src_ref, scale_ref, live_ref
        self.scores, self.peak, self.sums = scores_ref, peak_sc, sum_sc
        self.starts = range(0, blocks_ref.shape[0], LANES)

    def columns(self, at, size):
        depth = self.src.shape[1]
        columns = pl.ds(at, size)
        live = self.live[:, columns] > 0.5
        largest = []
        for start in self.starts:
            rows = pl.ds(start, LANES)
            product = lax.dot_general(
                self.blocks[rows, :depth], self.src[columns, :], (((1,), (1,)), ((), ())),
                preferred_element_type=jnp.float32,
            )
            scale = jnp.sum(self.blocks[rows, depth:].astype(jnp.float32), axis=1, keepdims=True)
            scores = jnp.where(scale > 0.0, product * scale * self.scale[:, columns], NEG_BIG)
            self.scores[rows, columns] = scores
            largest.append(jnp.max(scores, axis=0, keepdims=True))
            masked = jnp.where(live, scores, NEG_BIG)
            peak = fold(masked, jnp.maximum)
            if at:
                before = self.peak[rows, :]
                peak = jnp.maximum(before, peak)
            sums = functools.reduce(
                jnp.add, [jnp.exp2(masked[:, tile : tile + LANES] - peak) for tile in range(0, size, LANES)]
            )
            if at:
                sums = sums + self.sums[rows, :] * jnp.exp2(before - peak)
            self.peak[rows, :] = peak
            self.sums[rows, :] = sums
        return functools.reduce(jnp.maximum, largest)

    def exp_sums(self, at, size, row_max):
        columns = pl.ds(at, size)
        parts = [
            jnp.sum(jnp.exp2(self.scores[pl.ds(start, LANES), columns] - row_max), axis=0, keepdims=True)
            for start in self.starts
        ]
        return functools.reduce(jnp.add, parts)

    def logs(self, eye):
        rows = []
        for start in self.starts:
            peak = self.peak[pl.ds(start, LANES), :]
            highest = jnp.max(peak, axis=1, keepdims=True)
            total = jnp.sum(self.sums[pl.ds(start, LANES), :] * jnp.exp2(peak - highest), axis=1, keepdims=True)
            rows.append(column_to_row(highest + jnp.log(total) * LOG2_E, eye))
        return rows


def near_kernel(
    near_ref, src_ref, src_scale_ref, src_live_ref, scores_ref, row_max_ref, row_sum_ref, logs_ref, peak_sc, sum_sc
):
    half = Half(near_ref, src_ref, src_scale_ref, src_live_ref, scores_ref, peak_sc, sum_sc)
    sources = src_ref.shape[0]
    size = column_block(sources)
    for at in range(0, sources, size):
        row_max = half.columns(at, size)
        row_max_ref[:, pl.ds(at, size)] = row_max
        row_sum_ref[:, pl.ds(at, size)] = half.exp_sums(at, size, row_max)
    for row, values in enumerate(half.logs(diagonal(LANES))):
        logs_ref[pl.ds(row, 1), :] = values


def slot_lanes(phases, tgt_dev, row):
    me = lax.axis_index("blk")
    lane = lax.broadcasted_iota(jnp.int32, (1, LANES), 1)
    slot = (lane + row * LANES) // tgt_dev
    core_0 = (crossed(phases, slot) ^ (me & 1)) == 0
    return core_0, lane ^ ((own_slot(phases, me) * tgt_dev) & (LANES - 1))


def shared_row(phases, tgt_dev, row):
    return row ^ ((own_slot(phases, lax.axis_index("blk")) * tgt_dev) // LANES)


def permuted(row, lanes):
    shape = (8, LANES)
    lanes = jnp.broadcast_to(lanes, shape)
    return jnp.take_along_axis(jnp.broadcast_to(row, shape), lanes, axis=1)[:1, :]


def far_kernel(
    phases, tgt_dev,
    far_ref, src_ref, src_scale_ref, src_live_ref, near_scores_ref, near_max_ref, near_sum_ref, near_logs_ref,
    scores_ref, row_den_ref, stats_ref, peak_sc, sum_sc, near_best_sc, far_best_sc,
):
    half = Half(far_ref, src_ref, src_scale_ref, src_live_ref, scores_ref, peak_sc, sum_sc)
    sources = src_ref.shape[0]
    size = column_block(sources)
    for at in range(0, sources, size):
        columns = pl.ds(at, size)
        far_max = half.columns(at, size)
        near_max = near_max_ref[:, columns]
        row_max = jnp.maximum(near_max, far_max)
        row_sum = near_sum_ref[:, columns] * jnp.exp2(near_max - row_max) + half.exp_sums(at, size, row_max)
        row_den = row_max + jnp.log(row_sum) * LOG2_E
        row_den_ref[:, columns] = row_den
        taken = jnp.where(src_live_ref[:, columns] > 0.5, 0.5 * row_den, -NEG_BIG)
        for ref, best_sc in ((near_scores_ref, near_best_sc), (scores_ref, far_best_sc)):
            for start in half.starts:
                rows = pl.ds(start, LANES)
                best = fold(ref[rows, columns] - taken, jnp.maximum)
                best_sc[rows, :] = jnp.maximum(best_sc[rows, :], best) if at else best
    eye = diagonal(LANES)
    count = len(half.starts)
    logs = half.logs(eye)
    for row, start in enumerate(half.starts):
        rows = pl.ds(start, LANES)
        near_best, far_best = (
            column_to_row(jnp.max(best_sc[rows, :], axis=1, keepdims=True), eye)
            for best_sc in (near_best_sc, far_best_sc)
        )
        core_0, lanes = slot_lanes(phases, tgt_dev, row)
        place = shared_row(phases, tgt_dev, row)
        pairs = ((near_logs_ref[pl.ds(row, 1), :], logs[row]), (near_best, far_best))
        for kind, (near, far) in enumerate(pairs):
            for core, values in enumerate((jnp.where(core_0, near, far), jnp.where(core_0, far, near))):
                stats_ref[pl.ds((2 * kind + core) * count + place, 1), :] = permuted(values, lanes)


def merged(parts):
    highest = functools.reduce(jnp.maximum, parts)
    logs = highest + jnp.log(sum(jnp.exp2(part - highest) for part in parts)) * LOG2_E
    row = lax.broadcasted_iota(jnp.int32, highest.shape, 0)
    return jnp.where(row < highest.shape[0] // 2, logs, highest)


def finish_kernel(
    phases, tgt_dev, src_live_ref, own_live_ref, stats_ref, near_ref, far_ref, row_den_ref,
    best_source_hbm, best_target_hbm, source_sc, target_sc, sems,
):
    me = lax.axis_index("blk")
    sources = near_ref.shape[1]
    count = near_ref.shape[0] // LANES
    core, first = me & 1, own_slot(phases, me) * tgt_dev
    row = core * count + first // LANES
    best = stats_ref[pl.ds(2 * count + row, 1), :] - 0.5 * stats_ref[pl.ds(row, 1), :]
    lane = lax.broadcasted_iota(jnp.int32, (tgt_dev, LANES), 1)
    wanted = lax.broadcasted_iota(jnp.int32, (tgt_dev, LANES), 0) + (first & (LANES - 1))
    own = jnp.sum(jnp.where(lane == wanted, best * LN_2, 0.0), axis=1, keepdims=True)
    target_sc[...] = jnp.where(own_live_ref[...] > 0.5, column_to_row(own, diagonal(tgt_dev)), 0.0)
    target_copy = pltpu.make_async_copy(target_sc, best_target_hbm, sems.at[0])
    target_copy.start()
    eye = diagonal(LANES)
    row_best = jnp.full((1, sources), NEG_BIG, jnp.float32)
    for row in range(count):
        core_0, lanes = slot_lanes(phases, tgt_dev, row)
        place = shared_row(phases, tgt_dev, row)
        first = permuted(0.5 * stats_ref[pl.ds(place, 1), :], lanes)
        second = permuted(0.5 * stats_ref[pl.ds(count + place, 1), :], lanes)
        for ref, values in (
            (near_ref, jnp.where(core_0, first, second)),
            (far_ref, jnp.where(core_0, second, first)),
        ):
            margin = ref[pl.ds(row * LANES, LANES), :] - row_to_column(values, eye)
            row_best = jnp.maximum(row_best, jnp.max(margin, axis=0, keepdims=True))
    source_sc[...] = jnp.where(src_live_ref[...] > 0.5, (row_best - 0.5 * row_den_ref[...]) * LN_2, 0.0)
    source_copy = pltpu.make_async_copy(source_sc, best_source_hbm, sems.at[1])
    source_copy.start()
    target_copy.wait()
    source_copy.wait()


def mine(src_emb, src_scale, src_count, tgt_emb, tgt_scale, tgt_count):
    ranks = lax.axis_size("blk")
    params = pltpu.CompilerParams(vmem_limit_bytes=24 << 20)
    src_dev, depth = src_emb.shape
    tgt_dev = tgt_emb.shape[0]
    half = ranks // 2 * tgt_dev
    width = depth + LANES
    phases = exchange_phases(ranks)
    source_line = pltpu.VMEM((1, src_dev), jnp.float32)
    half_shape = pltpu.VMEM((half, src_dev), jnp.float32)
    near, own_live = pl.pallas_call(
        pack_kernel,
        out_shape=(pltpu.VMEM((tgt_dev, width), jnp.bfloat16), pltpu.VMEM((1, tgt_dev), jnp.float32)),
        in_specs=[SMEM, HBM, HBM],
        out_specs=(VMEM, VMEM),
        scratch_shapes=[
            pltpu.VMEM((1, tgt_dev), jnp.float32),
            pltpu.SemaphoreType.DMA((2,)),
        ],
        compiler_params=params,
        name="pack",
    )(tgt_count, in_hbm(tgt_emb), in_hbm(tgt_scale.reshape(1, tgt_dev)))
    load = pl.pallas_call(
        load_kernel,
        out_shape=(pltpu.VMEM((src_dev, depth), src_emb.dtype), source_line),
        in_specs=[HBM, HBM],
        out_specs=(VMEM, VMEM),
        scratch_shapes=[pltpu.SemaphoreType.DMA((2,))],
        compiler_params=params,
        cost_estimate=pl.CostEstimate(flops=0, bytes_accessed=2 * src_emb.size * 2, transcendentals=0),
        name="load",
    )
    sources, source_scales = load(in_hbm(src_emb), in_hbm(src_scale.reshape(1, src_dev)))
    sources_live = jnp.where(lax.broadcasted_iota(jnp.int32, (1, src_dev), 1) < src_count, 1.0, 0.0)
    for bits in phases:
        came = [exchange(near, ranks, mask) for mask in phase_masks(bits)]
        held, near = near, jnp.concatenate([near] + came, axis=0)
    early = exchange(jnp.concatenate([held, came[-1]], axis=0), ranks, 1)
    if len(came) > 1:
        late = exchange(jnp.concatenate(came[:-1], axis=0), ranks, 1)
        far = jnp.concatenate([early[: held.shape[0]], late, early[held.shape[0] :]], axis=0)
    else:
        far = early
    half_lanes = pltpu.VMEM((half, LANES), jnp.float32)
    near_scores, near_max, near_sum, near_logs = pl.pallas_call(
        near_kernel,
        out_shape=(half_shape, source_line, source_line, pltpu.VMEM((half // LANES, LANES), jnp.float32)),
        in_specs=[VMEM] * 4,
        out_specs=(VMEM,) * 4,
        scratch_shapes=[half_lanes] * 2,
        compiler_params=params,
        cost_estimate=pl.CostEstimate(
            flops=2 * half * src_dev * depth, bytes_accessed=4 * half * src_dev, transcendentals=2 * half * src_dev
        ),
        name="near",
    )(on_chip(near), on_chip(sources), on_chip(source_scales), on_chip(sources_live))
    far_scores, row_den, stats = pl.pallas_call(
        functools.partial(far_kernel, phases, tgt_dev),
        out_shape=(half_shape, source_line, pltpu.VMEM((4 * half // LANES, LANES), jnp.float32)),
        in_specs=[VMEM] * 8,
        out_specs=(VMEM,) * 3,
        scratch_shapes=[half_lanes] * 4,
        compiler_params=params,
        name="far",
    )(
        on_chip(far), on_chip(sources), on_chip(source_scales), on_chip(sources_live),
        on_chip(near_scores), on_chip(near_max), on_chip(near_sum), on_chip(near_logs),
    )
    stats = merged([stats, exchange(stats, ranks, 1)])
    for bits in phases:
        came = [exchange(stats, ranks, mask) for mask in phase_masks(bits)]
        stats = merged([stats] + came)
    best_source, best_target = pl.pallas_call(
        functools.partial(finish_kernel, phases, tgt_dev),
        out_shape=(
            pltpu.HBM((1, src_dev), jnp.float32),
            pltpu.HBM((1, tgt_dev), jnp.float32),
        ),
        in_specs=[VMEM] * 6,
        out_specs=(HBM, HBM),
        scratch_shapes=[
            pltpu.VMEM((1, src_dev), jnp.float32),
            pltpu.VMEM((1, tgt_dev), jnp.float32),
            pltpu.SemaphoreType.DMA((2,)),
        ],
        compiler_params=params,
        name="finish",
    )(
        on_chip(sources_live), on_chip(own_live), on_chip(stats), on_chip(near_scores), on_chip(far_scores),
        on_chip(row_den),
    )
    return best_source.reshape(src_dev), best_target.reshape(tgt_dev)


def solution(mesh):
    return jax.shard_map(
        mine,
        mesh=mesh,
        in_specs=(
            P(("pairs", "blk"), None),
            P(("pairs", "blk")),
            P(("pairs", "blk")),
            P(("pairs", "blk"), None),
            P(("pairs", "blk")),
            P(("pairs", "blk")),
        ),
        out_specs=(P(("pairs", "blk")), P(("pairs", "blk"))),
        check_vma=False,
    )
```

```python
import functools

import jax
import jax.numpy as jnp
from jax import lax
from jax.experimental import pallas as pl
from jax.experimental.pallas import tpu as pltpu
from jax.sharding import PartitionSpec as P


NEG_BIG = -1e30
LOG2_E = 1.4426950408889634
LN_2 = 0.6931471805599453
LANES = 128
SMEM = pl.BlockSpec(memory_space=pltpu.SMEM)
VMEM = pl.BlockSpec(memory_space=pltpu.VMEM)
HBM = pl.BlockSpec(memory_space=pltpu.HBM)


def exchange_phases(ranks):
    bits = list(range(ranks.bit_length() - 2, 0, -1))
    phases = [[bits.pop(0)]] if len(bits) % 2 else []
    return phases + [[low, high] for high, low in zip(bits[::2], bits[1::2])]


def phase_masks(bits):
    masks = [0]
    for bit in bits:
        masks = masks + [mask | (1 << bit) for mask in masks]
    return [mask | 1 for mask in masks[1:]]


def sends_ahead(phases, phase):
    return phase == 0 and len(phases) > 1 and len(phases[0]) == 1


def own_slot(phases, rank):
    place = 0
    for index, bit in enumerate(sum(phases, [])):
        place = place | (((rank >> bit) & 1) << index)
    return place


def crossed(phases, slot):
    crossing, index = 0, 0
    for bits in phases:
        part = (slot >> index) & ((1 << len(bits)) - 1)
        crossing = crossing ^ jnp.where(part != 0, 1, 0)
        index += len(bits)
    return crossing


def exchange(block, ranks, mask):
    return lax.ppermute(block, "blk", [(i, i ^ mask) for i in range(ranks)])


def on_chip(array):
    return pltpu.with_memory_space_constraint(array, pltpu.VMEM)


def in_hbm(array):
    return pltpu.with_memory_space_constraint(array, pltpu.HBM)


def diagonal(size):
    shape = (size, size)
    return lax.broadcasted_iota(jnp.int32, shape, 0) == lax.broadcasted_iota(jnp.int32, shape, 1)


def column_to_row(column, eye):
    return jnp.sum(jnp.where(eye, column, 0.0), axis=0, keepdims=True)


def row_to_column(row, eye):
    return jnp.sum(jnp.where(eye, row, 0.0), axis=1, keepdims=True)


def pack_kernel(count_ref, tgt_hbm, scale_hbm, packed_ref, live_ref, scale_ref, sems):
    rows, depth = tgt_hbm.shape
    copies = [
        pltpu.make_async_copy(scale_hbm, scale_ref, sems.at[0]),
        pltpu.make_async_copy(tgt_hbm, packed_ref.at[:, pl.ds(0, depth)], sems.at[1]),
    ]
    for copy in copies:
        copy.start()
    copies[0].wait()
    live = lax.broadcasted_iota(jnp.int32, (1, rows), 1) < count_ref[0]
    live_ref[...] = jnp.where(live, 1.0, 0.0)
    scale = row_to_column(jnp.where(live, scale_ref[...], 0.0), diagonal(rows))
    high = scale.astype(jnp.bfloat16).astype(jnp.float32)
    rest = scale - high
    middle = rest.astype(jnp.bfloat16).astype(jnp.float32)
    low = rest - middle
    lane = lax.broadcasted_iota(jnp.int32, (rows, LANES), 1)
    terms = jnp.where(lane == 0, high, jnp.where(lane == 1, middle, jnp.where(lane == 2, low, 0.0)))
    packed_ref[:, depth:] = terms.astype(jnp.bfloat16)
    copies[1].wait()


def load_kernel(src_hbm, scale_hbm, src_ref, scale_ref, sems):
    copies = [
        pltpu.make_async_copy(src_hbm, src_ref, sems.at[0]),
        pltpu.make_async_copy(scale_hbm, scale_ref, sems.at[1]),
    ]
    for copy in copies:
        copy.start()
    copies[1].wait()
    scale_ref[...] = scale_ref[...] * LOG2_E
    copies[0].wait()


def column_block(sources):
    return 4 * LANES if sources % (4 * LANES) == 0 else LANES


def fold(values, op):
    return functools.reduce(op, [values[:, at : at + LANES] for at in range(0, values.shape[1], LANES)])


class Half:
    def __init__(self, blocks_ref, src_ref, scale_ref, live_ref, scores_ref, peak_sc, sum_sc):
        self.blocks, self.src, self.scale, self.live = blocks_ref, src_ref, scale_ref, live_ref
        self.scores, self.peak, self.sums = scores_ref, peak_sc, sum_sc
        self.starts = range(0, blocks_ref.shape[0], LANES)

    def columns(self, at, size):
        depth = self.src.shape[1]
        columns = pl.ds(at, size)
        live = self.live[:, columns] > 0.5
        largest = []
        for start in self.starts:
            rows = pl.ds(start, LANES)
            product = lax.dot_general(
                self.blocks[rows, :depth], self.src[columns, :], (((1,), (1,)), ((), ())),
                preferred_element_type=jnp.float32,
            )
            scale = jnp.sum(self.blocks[rows, depth:].astype(jnp.float32), axis=1, keepdims=True)
            scores = jnp.where(scale > 0.0, product * scale * self.scale[:, columns], NEG_BIG)
            self.scores[rows, columns] = scores
            largest.append(jnp.max(scores, axis=0, keepdims=True))
            masked = jnp.where(live, scores, NEG_BIG)
            peak = fold(masked, jnp.maximum)
            if at:
                before = self.peak[rows, :]
                peak = jnp.maximum(before, peak)
            sums = functools.reduce(
                jnp.add, [jnp.exp2(masked[:, tile : tile + LANES] - peak) for tile in range(0, size, LANES)]
            )
            if at:
                sums = sums + self.sums[rows, :] * jnp.exp2(before - peak)
            self.peak[rows, :] = peak
            self.sums[rows, :] = sums
        return functools.reduce(jnp.maximum, largest)

    def exp_sums(self, at, size, row_max):
        columns = pl.ds(at, size)
        parts = [
            jnp.sum(jnp.exp2(self.scores[pl.ds(start, LANES), columns] - row_max), axis=0, keepdims=True)
            for start in self.starts
        ]
        return functools.reduce(jnp.add, parts)

    def logs(self, eye):
        rows = []
        for start in self.starts:
            peak = self.peak[pl.ds(start, LANES), :]
            highest = jnp.max(peak, axis=1, keepdims=True)
            total = jnp.sum(self.sums[pl.ds(start, LANES), :] * jnp.exp2(peak - highest), axis=1, keepdims=True)
            rows.append(column_to_row(highest + jnp.log(total) * LOG2_E, eye))
        return rows


def near_kernel(
    near_ref, src_ref, src_scale_ref, src_live_ref, scores_ref, row_max_ref, row_sum_ref, logs_ref, peak_sc, sum_sc
):
    half = Half(near_ref, src_ref, src_scale_ref, src_live_ref, scores_ref, peak_sc, sum_sc)
    sources = src_ref.shape[0]
    size = column_block(sources)
    for at in range(0, sources, size):
        row_max = half.columns(at, size)
        row_max_ref[:, pl.ds(at, size)] = row_max
        row_sum_ref[:, pl.ds(at, size)] = half.exp_sums(at, size, row_max)
    for row, values in enumerate(half.logs(diagonal(LANES))):
        logs_ref[pl.ds(row, 1), :] = values


def slot_lanes(phases, tgt_dev, row):
    me = lax.axis_index("blk")
    lane = lax.broadcasted_iota(jnp.int32, (1, LANES), 1)
    slot = (lane + row * LANES) // tgt_dev
    core_0 = (crossed(phases, slot) ^ (me & 1)) == 0
    return core_0, lane ^ ((own_slot(phases, me) * tgt_dev) & (LANES - 1))


def shared_row(phases, tgt_dev, row):
    return row ^ ((own_slot(phases, lax.axis_index("blk")) * tgt_dev) // LANES)


def permuted(row, lanes):
    shape = (8, LANES)
    lanes = jnp.broadcast_to(lanes, shape)
    return jnp.take_along_axis(jnp.broadcast_to(row, shape), lanes, axis=1)[:1, :]


def far_kernel(
    phases, tgt_dev,
    far_ref, src_ref, src_scale_ref, src_live_ref, near_scores_ref, near_max_ref, near_sum_ref, near_logs_ref,
    scores_ref, row_den_ref, stats_ref, peak_sc, sum_sc, near_best_sc, far_best_sc,
):
    half = Half(far_ref, src_ref, src_scale_ref, src_live_ref, scores_ref, peak_sc, sum_sc)
    sources = src_ref.shape[0]
    size = column_block(sources)
    for at in range(0, sources, size):
        columns = pl.ds(at, size)
        far_max = half.columns(at, size)
        near_max = near_max_ref[:, columns]
        row_max = jnp.maximum(near_max, far_max)
        row_sum = near_sum_ref[:, columns] * jnp.exp2(near_max - row_max) + half.exp_sums(at, size, row_max)
        row_den = row_max + jnp.log(row_sum) * LOG2_E
        row_den_ref[:, columns] = row_den
        taken = jnp.where(src_live_ref[:, columns] > 0.5, 0.5 * row_den, -NEG_BIG)
        for ref, best_sc in ((near_scores_ref, near_best_sc), (scores_ref, far_best_sc)):
            for start in half.starts:
                rows = pl.ds(start, LANES)
                best = fold(ref[rows, columns] - taken, jnp.maximum)
                best_sc[rows, :] = jnp.maximum(best_sc[rows, :], best) if at else best
    eye = diagonal(LANES)
    count = len(half.starts)
    logs = half.logs(eye)
    for row, start in enumerate(half.starts):
        rows = pl.ds(start, LANES)
        near_best, far_best = (
            column_to_row(jnp.max(best_sc[rows, :], axis=1, keepdims=True), eye)
            for best_sc in (near_best_sc, far_best_sc)
        )
        core_0, lanes = slot_lanes(phases, tgt_dev, row)
        place = shared_row(phases, tgt_dev, row)
        pairs = ((near_logs_ref[pl.ds(row, 1), :], logs[row]), (near_best, far_best))
        for kind, (near, far) in enumerate(pairs):
            for core, values in enumerate((jnp.where(core_0, near, far), jnp.where(core_0, far, near))):
                stats_ref[pl.ds((2 * kind + core) * count + place, 1), :] = permuted(values, lanes)


def merged(parts):
    highest = functools.reduce(jnp.maximum, parts)
    logs = highest + jnp.log(sum(jnp.exp2(part - highest) for part in parts)) * LOG2_E
    row = lax.broadcasted_iota(jnp.int32, highest.shape, 0)
    return jnp.where(row < highest.shape[0] // 2, logs, highest)


def finish_kernel(
    phases, tgt_dev, src_live_ref, own_live_ref, stats_ref, near_ref, far_ref, row_den_ref,
    best_source_hbm, best_target_hbm, source_sc, target_sc, sems,
):
    me = lax.axis_index("blk")
    sources = near_ref.shape[1]
    count = near_ref.shape[0] // LANES
    core, first = me & 1, own_slot(phases, me) * tgt_dev
    row = core * count + first // LANES
    best = stats_ref[pl.ds(2 * count + row, 1), :] - 0.5 * stats_ref[pl.ds(row, 1), :]
    lane = lax.broadcasted_iota(jnp.int32, (tgt_dev, LANES), 1)
    wanted = lax.broadcasted_iota(jnp.int32, (tgt_dev, LANES), 0) + (first & (LANES - 1))
    own = jnp.sum(jnp.where(lane == wanted, best * LN_2, 0.0), axis=1, keepdims=True)
    target_sc[...] = jnp.where(own_live_ref[...] > 0.5, column_to_row(own, diagonal(tgt_dev)), 0.0)
    target_copy = pltpu.make_async_copy(target_sc, best_target_hbm, sems.at[0])
    target_copy.start()
    eye = diagonal(LANES)
    row_best = jnp.full((1, sources), NEG_BIG, jnp.float32)
    for row in range(count):
        core_0, lanes = slot_lanes(phases, tgt_dev, row)
        place = shared_row(phases, tgt_dev, row)
        first = permuted(0.5 * stats_ref[pl.ds(place, 1), :], lanes)
        second = permuted(0.5 * stats_ref[pl.ds(count + place, 1), :], lanes)
        for ref, values in (
            (near_ref, jnp.where(core_0, first, second)),
            (far_ref, jnp.where(core_0, second, first)),
        ):
            margin = ref[pl.ds(row * LANES, LANES), :] - row_to_column(values, eye)
            row_best = jnp.maximum(row_best, jnp.max(margin, axis=0, keepdims=True))
    source_sc[...] = jnp.where(src_live_ref[...] > 0.5, (row_best - 0.5 * row_den_ref[...]) * LN_2, 0.0)
    source_copy = pltpu.make_async_copy(source_sc, best_source_hbm, sems.at[1])
    source_copy.start()
    target_copy.wait()
    source_copy.wait()


def mine(src_emb, src_scale, src_count, tgt_emb, tgt_scale, tgt_count):
    ranks = lax.axis_size("blk")
    params = pltpu.CompilerParams(vmem_limit_bytes=24 << 20)
    src_dev, depth = src_emb.shape
    tgt_dev = tgt_emb.shape[0]
    half = ranks // 2 * tgt_dev
    width = depth + LANES
    phases = exchange_phases(ranks)
    source_line = pltpu.VMEM((1, src_dev), jnp.float32)
    half_shape = pltpu.VMEM((half, src_dev), jnp.float32)
    near, own_live = pl.pallas_call(
        pack_kernel,
        out_shape=(pltpu.VMEM((tgt_dev, width), jnp.bfloat16), pltpu.VMEM((1, tgt_dev), jnp.float32)),
        in_specs=[SMEM, HBM, HBM],
        out_specs=(VMEM, VMEM),
        scratch_shapes=[
            pltpu.VMEM((1, tgt_dev), jnp.float32),
            pltpu.SemaphoreType.DMA((2,)),
        ],
        compiler_params=params,
        name="pack",
    )(tgt_count, in_hbm(tgt_emb), in_hbm(tgt_scale.reshape(1, tgt_dev)))
    load = pl.pallas_call(
        load_kernel,
        out_shape=(pltpu.VMEM((src_dev, depth), src_emb.dtype), source_line),
        in_specs=[HBM, HBM],
        out_specs=(VMEM, VMEM),
        scratch_shapes=[pltpu.SemaphoreType.DMA((2,))],
        compiler_params=params,
        cost_estimate=pl.CostEstimate(flops=0, bytes_accessed=2 * src_emb.size * 2, transcendentals=0),
        name="load",
    )
    sources, source_scales = load(in_hbm(src_emb), in_hbm(src_scale.reshape(1, src_dev)))
    sources_live = jnp.where(lax.broadcasted_iota(jnp.int32, (1, src_dev), 1) < src_count, 1.0, 0.0)
    ahead = None
    for phase, bits in enumerate(phases):
        masks = phase_masks(bits)
        if ahead is None:
            came = [exchange(near, ranks, mask) for mask in masks]
            if sends_ahead(phases, phase):
                ahead = exchange(near, ranks, phase_masks(phases[1])[0])
        else:
            rest = exchange(came[0], ranks, masks[0])
            came = [jnp.concatenate([ahead, rest], axis=0)] + [exchange(near, ranks, mask) for mask in masks[1:]]
            ahead = None
        held, near = near, jnp.concatenate([near] + came, axis=0)
    early = exchange(jnp.concatenate([held, came[-1]], axis=0), ranks, 1)
    if len(came) > 1:
        late = exchange(jnp.concatenate(came[:-1], axis=0), ranks, 1)
        far = jnp.concatenate([early[: held.shape[0]], late, early[held.shape[0] :]], axis=0)
    else:
        far = early
    half_lanes = pltpu.VMEM((half, LANES), jnp.float32)
    near_scores, near_max, near_sum, near_logs = pl.pallas_call(
        near_kernel,
        out_shape=(half_shape, source_line, source_line, pltpu.VMEM((half // LANES, LANES), jnp.float32)),
        in_specs=[VMEM] * 4,
        out_specs=(VMEM,) * 4,
        scratch_shapes=[half_lanes] * 2,
        compiler_params=params,
        cost_estimate=pl.CostEstimate(
            flops=2 * half * src_dev * depth, bytes_accessed=4 * half * src_dev, transcendentals=2 * half * src_dev
        ),
        name="near",
    )(on_chip(near), on_chip(sources), on_chip(source_scales), on_chip(sources_live))
    far_scores, row_den, stats = pl.pallas_call(
        functools.partial(far_kernel, phases, tgt_dev),
        out_shape=(half_shape, source_line, pltpu.VMEM((4 * half // LANES, LANES), jnp.float32)),
        in_specs=[VMEM] * 8,
        out_specs=(VMEM,) * 3,
        scratch_shapes=[half_lanes] * 4,
        compiler_params=params,
        name="far",
    )(
        on_chip(far), on_chip(sources), on_chip(source_scales), on_chip(sources_live),
        on_chip(near_scores), on_chip(near_max), on_chip(near_sum), on_chip(near_logs),
    )
    stats = merged([stats, exchange(stats, ranks, 1)])
    for bits in phases:
        came = [exchange(stats, ranks, mask) for mask in phase_masks(bits)]
        stats = merged([stats] + came)
    best_source, best_target = pl.pallas_call(
        functools.partial(finish_kernel, phases, tgt_dev),
        out_shape=(
            pltpu.HBM((1, src_dev), jnp.float32),
            pltpu.HBM((1, tgt_dev), jnp.float32),
        ),
        in_specs=[VMEM] * 6,
        out_specs=(HBM, HBM),
        scratch_shapes=[
            pltpu.VMEM((1, src_dev), jnp.float32),
            pltpu.VMEM((1, tgt_dev), jnp.float32),
            pltpu.SemaphoreType.DMA((2,)),
        ],
        compiler_params=params,
        name="finish",
    )(
        on_chip(sources_live), on_chip(own_live), on_chip(stats), on_chip(near_scores), on_chip(far_scores),
        on_chip(row_den),
    )
    return best_source.reshape(src_dev), best_target.reshape(tgt_dev)


def solution(mesh):
    return jax.shard_map(
        mine,
        mesh=mesh,
        in_specs=(
            P(("pairs", "blk"), None),
            P(("pairs", "blk")),
            P(("pairs", "blk")),
            P(("pairs", "blk"), None),
            P(("pairs", "blk")),
            P(("pairs", "blk")),
        ),
        out_specs=(P(("pairs", "blk")), P(("pairs", "blk"))),
        check_vma=False,
    )
```

```python
import functools

import jax
import jax.numpy as jnp
from jax import lax
from jax.experimental import pallas as pl
from jax.experimental.pallas import tpu as pltpu
from jax.sharding import PartitionSpec as P


NEG_BIG = -1e30
LOG2_E = 1.4426950408889634
LN_2 = 0.6931471805599453
LANES = 128
SMEM = pl.BlockSpec(memory_space=pltpu.SMEM)
VMEM = pl.BlockSpec(memory_space=pltpu.VMEM)
HBM = pl.BlockSpec(memory_space=pltpu.HBM)


def exchange_phases(ranks):
    bits = list(range(ranks.bit_length() - 2, 0, -1))
    phases = [[bits.pop(0)]] if len(bits) % 2 else []
    return phases + [[low, high] for high, low in zip(bits[::2], bits[1::2])]


def phase_masks(bits):
    masks = [0]
    for bit in bits:
        masks = masks + [mask | (1 << bit) for mask in masks]
    return [mask | 1 for mask in masks[1:]]


def masks_ahead(phases):
    if len(phases) < 2 or len(phases[0]) > 1:
        return []
    masks = phase_masks(phases[1])
    return [masks[-1], masks[0]]


def own_slot(phases, rank):
    place = 0
    for index, bit in enumerate(sum(phases, [])):
        place = place | (((rank >> bit) & 1) << index)
    return place


def crossed(phases, slot):
    crossing, index = 0, 0
    for bits in phases:
        part = (slot >> index) & ((1 << len(bits)) - 1)
        crossing = crossing ^ jnp.where(part != 0, 1, 0)
        index += len(bits)
    return crossing


def exchange(block, ranks, mask):
    return lax.ppermute(block, "blk", [(i, i ^ mask) for i in range(ranks)])


def on_chip(array):
    return pltpu.with_memory_space_constraint(array, pltpu.VMEM)


def in_hbm(array):
    return pltpu.with_memory_space_constraint(array, pltpu.HBM)


def diagonal(size):
    shape = (size, size)
    return lax.broadcasted_iota(jnp.int32, shape, 0) == lax.broadcasted_iota(jnp.int32, shape, 1)


def column_to_row(column, eye):
    return jnp.sum(jnp.where(eye, column, 0.0), axis=0, keepdims=True)


def row_to_column(row, eye):
    return jnp.sum(jnp.where(eye, row, 0.0), axis=1, keepdims=True)


def pack_kernel(count_ref, tgt_hbm, scale_hbm, packed_ref, live_ref, scale_ref, sems):
    rows, depth = tgt_hbm.shape
    copies = [
        pltpu.make_async_copy(scale_hbm, scale_ref, sems.at[0]),
        pltpu.make_async_copy(tgt_hbm, packed_ref.at[:, pl.ds(0, depth)], sems.at[1]),
    ]
    for copy in copies:
        copy.start()
    copies[0].wait()
    live = lax.broadcasted_iota(jnp.int32, (1, rows), 1) < count_ref[0]
    live_ref[...] = jnp.where(live, 1.0, 0.0)
    scale = row_to_column(jnp.where(live, scale_ref[...], 0.0), diagonal(rows))
    high = scale.astype(jnp.bfloat16).astype(jnp.float32)
    rest = scale - high
    middle = rest.astype(jnp.bfloat16).astype(jnp.float32)
    low = rest - middle
    lane = lax.broadcasted_iota(jnp.int32, (rows, LANES), 1)
    terms = jnp.where(lane == 0, high, jnp.where(lane == 1, middle, jnp.where(lane == 2, low, 0.0)))
    packed_ref[:, depth:] = terms.astype(jnp.bfloat16)
    copies[1].wait()


def load_kernel(src_hbm, scale_hbm, src_ref, scale_ref, sems):
    copies = [
        pltpu.make_async_copy(src_hbm, src_ref, sems.at[0]),
        pltpu.make_async_copy(scale_hbm, scale_ref, sems.at[1]),
    ]
    for copy in copies:
        copy.start()
    copies[1].wait()
    scale_ref[...] = scale_ref[...] * LOG2_E
    copies[0].wait()


def column_block(sources):
    return 4 * LANES if sources % (4 * LANES) == 0 else LANES


def fold(values, op):
    return functools.reduce(op, [values[:, at : at + LANES] for at in range(0, values.shape[1], LANES)])


class Half:
    def __init__(self, blocks_ref, src_ref, scale_ref, live_ref, scores_ref, peak_sc, sum_sc):
        self.blocks, self.src, self.scale, self.live = blocks_ref, src_ref, scale_ref, live_ref
        self.scores, self.peak, self.sums = scores_ref, peak_sc, sum_sc
        self.starts = range(0, blocks_ref.shape[0], LANES)

    def columns(self, at, size):
        depth = self.src.shape[1]
        columns = pl.ds(at, size)
        live = self.live[:, columns] > 0.5
        largest = []
        for start in self.starts:
            rows = pl.ds(start, LANES)
            product = lax.dot_general(
                self.blocks[rows, :depth], self.src[columns, :], (((1,), (1,)), ((), ())),
                preferred_element_type=jnp.float32,
            )
            scale = jnp.sum(self.blocks[rows, depth:].astype(jnp.float32), axis=1, keepdims=True)
            scores = jnp.where(scale > 0.0, product * scale * self.scale[:, columns], NEG_BIG)
            self.scores[rows, columns] = scores
            largest.append(jnp.max(scores, axis=0, keepdims=True))
            masked = jnp.where(live, scores, NEG_BIG)
            peak = fold(masked, jnp.maximum)
            if at:
                before = self.peak[rows, :]
                peak = jnp.maximum(before, peak)
            sums = functools.reduce(
                jnp.add, [jnp.exp2(masked[:, tile : tile + LANES] - peak) for tile in range(0, size, LANES)]
            )
            if at:
                sums = sums + self.sums[rows, :] * jnp.exp2(before - peak)
            self.peak[rows, :] = peak
            self.sums[rows, :] = sums
        return functools.reduce(jnp.maximum, largest)

    def exp_sums(self, at, size, row_max):
        columns = pl.ds(at, size)
        parts = [
            jnp.sum(jnp.exp2(self.scores[pl.ds(start, LANES), columns] - row_max), axis=0, keepdims=True)
            for start in self.starts
        ]
        return functools.reduce(jnp.add, parts)

    def logs(self, eye):
        rows = []
        for start in self.starts:
            peak = self.peak[pl.ds(start, LANES), :]
            highest = jnp.max(peak, axis=1, keepdims=True)
            total = jnp.sum(self.sums[pl.ds(start, LANES), :] * jnp.exp2(peak - highest), axis=1, keepdims=True)
            rows.append(column_to_row(highest + jnp.log(total) * LOG2_E, eye))
        return rows


def near_kernel(
    near_ref, src_ref, src_scale_ref, src_live_ref, scores_ref, row_max_ref, row_sum_ref, logs_ref, peak_sc, sum_sc
):
    half = Half(near_ref, src_ref, src_scale_ref, src_live_ref, scores_ref, peak_sc, sum_sc)
    sources = src_ref.shape[0]
    size = column_block(sources)
    for at in range(0, sources, size):
        row_max = half.columns(at, size)
        row_max_ref[:, pl.ds(at, size)] = row_max
        row_sum_ref[:, pl.ds(at, size)] = half.exp_sums(at, size, row_max)
    for row, values in enumerate(half.logs(diagonal(LANES))):
        logs_ref[pl.ds(row, 1), :] = values


def slot_lanes(phases, tgt_dev, row):
    me = lax.axis_index("blk")
    lane = lax.broadcasted_iota(jnp.int32, (1, LANES), 1)
    slot = (lane + row * LANES) // tgt_dev
    core_0 = (crossed(phases, slot) ^ (me & 1)) == 0
    return core_0, lane ^ ((own_slot(phases, me) * tgt_dev) & (LANES - 1))


def shared_row(phases, tgt_dev, row):
    return row ^ ((own_slot(phases, lax.axis_index("blk")) * tgt_dev) // LANES)


def permuted(row, lanes):
    shape = (8, LANES)
    lanes = jnp.broadcast_to(lanes, shape)
    return jnp.take_along_axis(jnp.broadcast_to(row, shape), lanes, axis=1)[:1, :]


def far_kernel(
    phases, tgt_dev,
    far_ref, src_ref, src_scale_ref, src_live_ref, near_scores_ref, near_max_ref, near_sum_ref, near_logs_ref,
    scores_ref, row_den_ref, stats_ref, peak_sc, sum_sc, near_best_sc, far_best_sc,
):
    half = Half(far_ref, src_ref, src_scale_ref, src_live_ref, scores_ref, peak_sc, sum_sc)
    sources = src_ref.shape[0]
    size = column_block(sources)
    for at in range(0, sources, size):
        columns = pl.ds(at, size)
        far_max = half.columns(at, size)
        near_max = near_max_ref[:, columns]
        row_max = jnp.maximum(near_max, far_max)
        row_sum = near_sum_ref[:, columns] * jnp.exp2(near_max - row_max) + half.exp_sums(at, size, row_max)
        row_den = row_max + jnp.log(row_sum) * LOG2_E
        row_den_ref[:, columns] = row_den
        taken = jnp.where(src_live_ref[:, columns] > 0.5, 0.5 * row_den, -NEG_BIG)
        for ref, best_sc in ((near_scores_ref, near_best_sc), (scores_ref, far_best_sc)):
            for start in half.starts:
                rows = pl.ds(start, LANES)
                best = fold(ref[rows, columns] - taken, jnp.maximum)
                best_sc[rows, :] = jnp.maximum(best_sc[rows, :], best) if at else best
    eye = diagonal(LANES)
    count = len(half.starts)
    logs = half.logs(eye)
    for row, start in enumerate(half.starts):
        rows = pl.ds(start, LANES)
        near_best, far_best = (
            column_to_row(jnp.max(best_sc[rows, :], axis=1, keepdims=True), eye)
            for best_sc in (near_best_sc, far_best_sc)
        )
        core_0, lanes = slot_lanes(phases, tgt_dev, row)
        place = shared_row(phases, tgt_dev, row)
        pairs = ((near_logs_ref[pl.ds(row, 1), :], logs[row]), (near_best, far_best))
        for kind, (near, far) in enumerate(pairs):
            for core, values in enumerate((jnp.where(core_0, near, far), jnp.where(core_0, far, near))):
                stats_ref[pl.ds((2 * kind + core) * count + place, 1), :] = permuted(values, lanes)


def merged(parts):
    highest = functools.reduce(jnp.maximum, parts)
    logs = highest + jnp.log(sum(jnp.exp2(part - highest) for part in parts)) * LOG2_E
    row = lax.broadcasted_iota(jnp.int32, highest.shape, 0)
    return jnp.where(row < highest.shape[0] // 2, logs, highest)


def finish_kernel(
    phases, tgt_dev, src_live_ref, own_live_ref, stats_ref, near_ref, far_ref, row_den_ref,
    best_source_hbm, best_target_hbm, source_sc, target_sc, sems,
):
    me = lax.axis_index("blk")
    sources = near_ref.shape[1]
    count = near_ref.shape[0] // LANES
    core, first = me & 1, own_slot(phases, me) * tgt_dev
    row = core * count + first // LANES
    best = stats_ref[pl.ds(2 * count + row, 1), :] - 0.5 * stats_ref[pl.ds(row, 1), :]
    lane = lax.broadcasted_iota(jnp.int32, (tgt_dev, LANES), 1)
    wanted = lax.broadcasted_iota(jnp.int32, (tgt_dev, LANES), 0) + (first & (LANES - 1))
    own = jnp.sum(jnp.where(lane == wanted, best * LN_2, 0.0), axis=1, keepdims=True)
    target_sc[...] = jnp.where(own_live_ref[...] > 0.5, column_to_row(own, diagonal(tgt_dev)), 0.0)
    target_copy = pltpu.make_async_copy(target_sc, best_target_hbm, sems.at[0])
    target_copy.start()
    eye = diagonal(LANES)
    row_best = jnp.full((1, sources), NEG_BIG, jnp.float32)
    for row in range(count):
        core_0, lanes = slot_lanes(phases, tgt_dev, row)
        place = shared_row(phases, tgt_dev, row)
        first = permuted(0.5 * stats_ref[pl.ds(place, 1), :], lanes)
        second = permuted(0.5 * stats_ref[pl.ds(count + place, 1), :], lanes)
        for ref, values in (
            (near_ref, jnp.where(core_0, first, second)),
            (far_ref, jnp.where(core_0, second, first)),
        ):
            margin = ref[pl.ds(row * LANES, LANES), :] - row_to_column(values, eye)
            row_best = jnp.maximum(row_best, jnp.max(margin, axis=0, keepdims=True))
    source_sc[...] = jnp.where(src_live_ref[...] > 0.5, (row_best - 0.5 * row_den_ref[...]) * LN_2, 0.0)
    source_copy = pltpu.make_async_copy(source_sc, best_source_hbm, sems.at[1])
    source_copy.start()
    target_copy.wait()
    source_copy.wait()


def mine(src_emb, src_scale, src_count, tgt_emb, tgt_scale, tgt_count):
    ranks = lax.axis_size("blk")
    params = pltpu.CompilerParams(vmem_limit_bytes=24 << 20)
    src_dev, depth = src_emb.shape
    tgt_dev = tgt_emb.shape[0]
    half = ranks // 2 * tgt_dev
    width = depth + LANES
    phases = exchange_phases(ranks)
    source_line = pltpu.VMEM((1, src_dev), jnp.float32)
    half_shape = pltpu.VMEM((half, src_dev), jnp.float32)
    near, own_live = pl.pallas_call(
        pack_kernel,
        out_shape=(pltpu.VMEM((tgt_dev, width), jnp.bfloat16), pltpu.VMEM((1, tgt_dev), jnp.float32)),
        in_specs=[SMEM, HBM, HBM],
        out_specs=(VMEM, VMEM),
        scratch_shapes=[
            pltpu.VMEM((1, tgt_dev), jnp.float32),
            pltpu.SemaphoreType.DMA((2,)),
        ],
        compiler_params=params,
        name="pack",
    )(tgt_count, in_hbm(tgt_emb), in_hbm(tgt_scale.reshape(1, tgt_dev)))
    load = pl.pallas_call(
        load_kernel,
        out_shape=(pltpu.VMEM((src_dev, depth), src_emb.dtype), source_line),
        in_specs=[HBM, HBM],
        out_specs=(VMEM, VMEM),
        scratch_shapes=[pltpu.SemaphoreType.DMA((2,))],
        compiler_params=params,
        cost_estimate=pl.CostEstimate(flops=0, bytes_accessed=2 * src_emb.size * 2, transcendentals=0),
        name="load",
    )
    sources, source_scales = load(in_hbm(src_emb), in_hbm(src_scale.reshape(1, src_dev)))
    sources_live = jnp.where(lax.broadcasted_iota(jnp.int32, (1, src_dev), 1) < src_count, 1.0, 0.0)
    ahead = {}
    for phase, bits in enumerate(phases):
        masks = phase_masks(bits)
        sent_ahead, ahead = ahead, {}
        if sent_ahead:
            blocks = came[0]
        came = [
            jnp.concatenate([sent_ahead[mask], exchange(blocks, ranks, mask)], axis=0)
            if mask in sent_ahead
            else exchange(near, ranks, mask)
            for mask in masks
        ]
        if phase == 0:
            ahead = {mask: exchange(near, ranks, mask) for mask in masks_ahead(phases)}
        held, near = near, jnp.concatenate([near] + came, axis=0)
    early = exchange(jnp.concatenate([held, came[-1]], axis=0), ranks, 1)
    if len(came) > 1:
        late = exchange(jnp.concatenate(came[:-1], axis=0), ranks, 1)
        far = jnp.concatenate([early[: held.shape[0]], late, early[held.shape[0] :]], axis=0)
    else:
        far = early
    half_lanes = pltpu.VMEM((half, LANES), jnp.float32)
    near_scores, near_max, near_sum, near_logs = pl.pallas_call(
        near_kernel,
        out_shape=(half_shape, source_line, source_line, pltpu.VMEM((half // LANES, LANES), jnp.float32)),
        in_specs=[VMEM] * 4,
        out_specs=(VMEM,) * 4,
        scratch_shapes=[half_lanes] * 2,
        compiler_params=params,
        cost_estimate=pl.CostEstimate(
            flops=2 * half * src_dev * depth, bytes_accessed=4 * half * src_dev, transcendentals=2 * half * src_dev
        ),
        name="near",
    )(on_chip(near), on_chip(sources), on_chip(source_scales), on_chip(sources_live))
    far_scores, row_den, stats = pl.pallas_call(
        functools.partial(far_kernel, phases, tgt_dev),
        out_shape=(half_shape, source_line, pltpu.VMEM((4 * half // LANES, LANES), jnp.float32)),
        in_specs=[VMEM] * 8,
        out_specs=(VMEM,) * 3,
        scratch_shapes=[half_lanes] * 4,
        compiler_params=params,
        name="far",
    )(
        on_chip(far), on_chip(sources), on_chip(source_scales), on_chip(sources_live),
        on_chip(near_scores), on_chip(near_max), on_chip(near_sum), on_chip(near_logs),
    )
    stats = merged([stats, exchange(stats, ranks, 1)])
    for bits in phases:
        came = [exchange(stats, ranks, mask) for mask in phase_masks(bits)]
        stats = merged([stats] + came)
    best_source, best_target = pl.pallas_call(
        functools.partial(finish_kernel, phases, tgt_dev),
        out_shape=(
            pltpu.HBM((1, src_dev), jnp.float32),
            pltpu.HBM((1, tgt_dev), jnp.float32),
        ),
        in_specs=[VMEM] * 6,
        out_specs=(HBM, HBM),
        scratch_shapes=[
            pltpu.VMEM((1, src_dev), jnp.float32),
            pltpu.VMEM((1, tgt_dev), jnp.float32),
            pltpu.SemaphoreType.DMA((2,)),
        ],
        compiler_params=params,
        name="finish",
    )(
        on_chip(sources_live), on_chip(own_live), on_chip(stats), on_chip(near_scores), on_chip(far_scores),
        on_chip(row_den),
    )
    return best_source.reshape(src_dev), best_target.reshape(tgt_dev)


def solution(mesh):
    return jax.shard_map(
        mine,
        mesh=mesh,
        in_specs=(
            P(("pairs", "blk"), None),
            P(("pairs", "blk")),
            P(("pairs", "blk")),
            P(("pairs", "blk"), None),
            P(("pairs", "blk")),
            P(("pairs", "blk")),
        ),
        out_specs=(P(("pairs", "blk")), P(("pairs", "blk"))),
        check_vma=False,
    )
```
